128 devices in a mesh: gx: 32 (over z, y, x_hi), gy: 4 (over x_lo, core).
Axes of the slice: x: 4 (x_hi: 2, x_lo: 2; x = x_hi * 2 + x_lo), y: 4, z: 4, core: 2. Of those that a mesh axis runs over, the one named last changes fastest.
Arguments:
- populations: float32 [27, 128, 64, 256], P(None, 'gx', 'gy'), may hold values from 0.4 to 1.6
- omega: float32 [128, 64, 256], P('gx', 'gy'), may hold values from 1.2 to 1.9
- walls: int32 [128, 64, 256], P('gx', 'gy'), may hold values 0 or 1
- radiation: bfloat16 [4096, 512], replicated, may hold values from -0.25 to 0.25
- bins: int32 [512, 32], replicated, may hold values from 0 to 126
- counts: int32 [32, 4], P('gx', 'gy'), may hold values from 1 to 16, as said below
- sample_site: int32 [32, 4, 16], P('gx', 'gy'), may hold values from 0 to 127, as said below
- sample_patch: int32 [32, 4, 16], P('gx', 'gy'), may hold values from 0 to 511, as said below
Outputs:
- advanced: float32 [27, 128, 64, 256], P(None, 'gx', 'gy')
- signal: float32 [4096, 128], P(('gx', 'gy'))
The draws below stay inside these ranges and needn't reach their ends.
Inputs may be any that keep to these rules, and one draw needn't show every extreme that they name: `counts`: live samples fill a device's first slots; some device has all 16. `sample_site`: site numbers of one device are distinct. `sample_patch`: a device with gy index j names only patches j * 128 to (j + 1) * 128 - 1.
All inputs are finite; a program needn't handle non-finite values. No bound on the sum of `walls` on one device may be relied on, other than what follows from the above.
Results may differ from the reference program's by a relative error of at most 0.0037.
Values may be sent and summed in bfloat16 or wider, within the bound.
A program may use at most 64 MiB of HBM per device.

```python
import jax
import jax.numpy as jnp
from jax import lax

CX = 4
CY = 16
NZ = 256
ZS = 128
SAMP = 16
OBS = 4096
OBS_BLK = 128
LEVELS = 128
STEPS = 2
NX = 128
NY = 64
SITES = 128
PCOL = 128
PATCHES = 512
OBLK = 32
N_GX = 32
N_GY = 4


def draw_counts(key, part):
    drawn = jax.random.randint(key, (N_GX * N_GY,), 1, SAMP + 1)
    chosen_device = jax.random.randint(jax.random.fold_in(key, 7), (), 0, N_GX * N_GY)
    filled = jnp.where(jnp.arange(N_GX * N_GY) == chosen_device, SAMP, drawn)
    return filled.reshape(N_GX, N_GY).astype(jnp.int32)


def draw_sample_site(key, part):
    device_keys = jax.random.split(key, N_GX * N_GY)
    picked = jax.vmap(lambda device_key: jax.random.permutation(device_key, SITES)[:SAMP])(device_keys)
    return picked.reshape(N_GX, N_GY, SAMP).astype(jnp.int32)


def draw_sample_patch(key, part):
    drawn = jax.random.randint(key, (N_GX, N_GY, SAMP), 0, PCOL)
    offset = jnp.arange(N_GY)[None, :, None] * PCOL
    patches = (drawn + offset).astype(jnp.int32)
    patches = patches.at[0, 0, 0].set(0)
    patches = patches.at[0, N_GY - 1, 0].set(PATCHES - 1)
    return patches.astype(jnp.int32)


def place_ends(values, stream_key, smallest, largest):
    shape = values.shape
    index_at = [jax.random.randint(jax.random.fold_in(stream_key, axis), (), 0, shape[axis]) for axis in range(len(shape))]
    values = values.at[tuple(index_at)].set(smallest)
    longest = shape.index(max(shape))
    index_at[longest] = (index_at[longest] + 1) % shape[longest]
    return values.at[tuple(index_at)].set(largest)


def block_levels(stream_key, dims, shards, least, largest):
    gain = 1.0
    for dim, parts in shards:
        steps = jax.random.uniform(jax.random.fold_in(jax.random.fold_in(stream_key, 6), dim), (parts,), jnp.float32, least / len(shards), largest / len(shards))
        gain = gain * jnp.repeat(jnp.exp(steps), dims[dim] // parts).reshape((-1,) + (1,) * (len(dims) - 1 - dim))
    return gain


def gaussian(stream_key, shape, spread, most, kind=jnp.bfloat16):
    values = jax.random.normal(stream_key, shape, jnp.float32) * spread
    return jnp.minimum(jnp.maximum(values, -most), most).astype(kind)


def setup_inputs(seed: int = 0) -> dict:
    arg_keys = jax.random.split(jax.random.key(seed), 9)
    return {
        "populations": jnp.clip(0.4 + 1.2 * jax.random.uniform(arg_keys[0], (27, NX, NY, NZ), jnp.float32) ** block_levels(arg_keys[0], (27, NX, NY, NZ), ((1, 32), (2, 4)), -0.2, 0.2), 0.4, 1.6),
        "omega": jnp.clip(1.2 + 0.6999999 * jax.random.uniform(arg_keys[1], (NX, NY, NZ), jnp.float32) ** block_levels(arg_keys[1], (NX, NY, NZ), ((0, 32), (1, 4)), -0.2, 0.2), 1.2, 1.9),
        "walls": place_ends((jax.random.randint(arg_keys[2], (NX, NY, NZ), 0, 8) < 1).astype(jnp.int32), jax.random.fold_in(arg_keys[2], 1), 0, 1),
        "radiation": gaussian(arg_keys[3], (OBS, 4 * ZS), (4 * ZS) ** -0.5, 0.25),
        "bins": place_ends(jax.random.randint(arg_keys[4], (PATCHES, OBLK), 0, LEVELS - STEPS + 1), jax.random.fold_in(arg_keys[4], 1), 0, LEVELS - STEPS).astype(jnp.int32),
        "counts": draw_counts(jax.random.fold_in(arg_keys[8], 71), 0),
        "sample_site": draw_sample_site(jax.random.fold_in(arg_keys[8], 71), 0),
        "sample_patch": draw_sample_patch(jax.random.fold_in(arg_keys[8], 71), 0),
    }


def lattice_weight():
    values = []
    for direction in range(27):
        moving = int(direction // 9 != 1) + int((direction // 3) % 3 != 1) + int(direction % 3 != 1)
        values.append([8.0 / 27.0, 2.0 / 27.0, 1.0 / 54.0, 1.0 / 216.0][moving])
    return jnp.array(values, dtype=jnp.float32)


def forward(lattice, axis_index, velocity):
    rotated = jnp.moveaxis(lattice, axis_index, 0)
    minus_side, centre, plus_side = rotated[0], rotated[1], rotated[2]
    summed = minus_side + centre + plus_side
    difference = plus_side - minus_side
    first_order = difference - velocity * summed
    second_order = plus_side + minus_side - 2.0 * velocity * difference + velocity * velocity * summed
    return jnp.moveaxis(jnp.stack([summed, first_order, second_order]), 0, axis_index)


def backward(lattice, axis_index, velocity):
    rotated = jnp.moveaxis(lattice, axis_index, 0)
    order_zero, order_one, order_two = rotated[0], rotated[1], rotated[2]
    difference = order_one + velocity * order_zero
    summed_ends = order_two + 2.0 * velocity * order_one + velocity * velocity * order_zero
    minus_side = 0.5 * (summed_ends - difference)
    plus_side = 0.5 * (summed_ends + difference)
    centre = order_zero - summed_ends
    return jnp.moveaxis(jnp.stack([minus_side, centre, plus_side]), 0, axis_index)


def collide(distribution, omega):
    trailing = distribution.shape[1:]
    lattice = distribution.reshape((3, 3, 3) + trailing)
    density = jnp.sum(lattice, axis=(0, 1, 2))
    vel_x = jnp.sum(lattice[2] - lattice[0], axis=(0, 1)) / density
    vel_y = jnp.sum(lattice[:, 2] - lattice[:, 0], axis=(0, 1)) / density
    vel_z = jnp.sum(lattice[:, :, 2] - lattice[:, :, 0], axis=(0, 1)) / density
    moments = forward(lattice, 2, vel_z)
    moments = forward(moments, 1, vel_y)
    moments = forward(moments, 0, vel_x)
    retain = 1.0 - omega
    normal_xy = retain * (moments[2, 0, 0] - moments[0, 2, 0])
    normal_xz = retain * (moments[2, 0, 0] - moments[0, 0, 2])
    post_xx = (density + normal_xy + normal_xz) / 3.0
    post_yy = (density - 2.0 * normal_xy + normal_xz) / 3.0
    post_zz = (density + normal_xy - 2.0 * normal_xz) / 3.0
    post_xy = retain * moments[1, 1, 0]
    post_xz = retain * moments[1, 0, 1]
    post_yz = retain * moments[0, 1, 1]
    inverse = 1.0 / density
    entries = {
        (0, 0, 0): density,
        (2, 0, 0): post_xx,
        (0, 2, 0): post_yy,
        (0, 0, 2): post_zz,
        (1, 1, 0): post_xy,
        (1, 0, 1): post_xz,
        (0, 1, 1): post_yz,
        (2, 2, 0): (post_xx * post_yy + 2.0 * post_xy * post_xy) * inverse,
        (2, 0, 2): (post_xx * post_zz + 2.0 * post_xz * post_xz) * inverse,
        (0, 2, 2): (post_yy * post_zz + 2.0 * post_yz * post_yz) * inverse,
        (2, 1, 1): (post_xx * post_yz + 2.0 * post_xy * post_xz) * inverse,
        (1, 2, 1): (post_yy * post_xz + 2.0 * post_xy * post_yz) * inverse,
        (1, 1, 2): (post_zz * post_xy + 2.0 * post_xz * post_yz) * inverse,
        (2, 2, 2): (post_xx * post_yy * post_zz + 2.0 * post_xx * post_yz * post_yz
                    + 2.0 * post_yy * post_xz * post_xz + 2.0 * post_zz * post_xy * post_xy
                    + 8.0 * post_xy * post_xz * post_yz) * inverse * inverse,
    }
    nothing = jnp.zeros_like(density)
    listed = [entries.get((order_x, order_y, order_z), nothing)
              for order_x in range(3) for order_y in range(3) for order_z in range(3)]
    relaxed = jnp.stack(listed).reshape((3, 3, 3) + trailing)
    relaxed = backward(relaxed, 0, vel_x)
    relaxed = backward(relaxed, 1, vel_y)
    relaxed = backward(relaxed, 2, vel_z)
    return relaxed.reshape((27,) + trailing)


def macro_rows(read):
    lattice = read.reshape((3, 3, 3) + read.shape[1:])
    density = jnp.sum(lattice, axis=(0, 1, 2))
    mom_x = jnp.sum(lattice[2] - lattice[0], axis=(0, 1))
    mom_y = jnp.sum(lattice[:, 2] - lattice[:, 0], axis=(0, 1))
    mom_z = jnp.sum(lattice[:, :, 2] - lattice[:, :, 0], axis=(0, 1))
    return jnp.stack([density - 1.0, mom_x, mom_y, mom_z])


def radiate(read, radiation, bins, counts, sample_site, sample_patch, step_index):
    fields = macro_rows(read).reshape(4, NX, NY, NZ // ZS, ZS)
    local_x = sample_site // (CY * (NZ // ZS))
    local_y = (sample_site // (NZ // ZS)) % CY
    segment = sample_site % (NZ // ZS)
    global_x = jnp.arange(N_GX, dtype=jnp.int32)[:, None, None] * CX + local_x
    global_y = jnp.arange(N_GY, dtype=jnp.int32)[None, :, None] * CY + local_y
    picked = fields[:, global_x, global_y, segment, :]
    picked = jnp.moveaxis(picked, 0, 3).reshape(N_GX * N_GY * SAMP, 4 * ZS)
    live_slot = (jnp.arange(SAMP, dtype=jnp.int32)[None, None, :] < counts[:, :, None]).reshape(-1)
    surface = jnp.where(live_slot[:, None], picked, 0.0).astype(jnp.bfloat16)
    patch_sum = jax.ops.segment_sum(surface.astype(jnp.float32), sample_patch.reshape(-1), num_segments=PATCHES)
    response = lax.dot_general(radiation, patch_sum.astype(jnp.bfloat16), (((1,), (1,)), ((), ())),
                               preferred_element_type=jnp.float32)
    levels_hit = bins + step_index
    one_hot = (levels_hit[:, :, None] == jnp.arange(LEVELS, dtype=jnp.int32)).astype(jnp.float32)
    binned = jnp.einsum("bop,pbl->bol", response.reshape(OBS // OBS_BLK, OBS_BLK, PATCHES), one_hot,
                        precision=lax.Precision.HIGHEST)
    return binned.reshape(OBS, LEVELS)


def reference(populations, omega, walls, radiation, bins, counts, sample_site, sample_patch):
    weight = lattice_weight()[:, None, None, None]
    solid_cell = walls == 1
    current = populations
    signal = jnp.zeros((OBS, LEVELS), jnp.float32)
    for step_index in range(STEPS):
        before = current * weight
        planes = lax.map(lambda plane_pair: collide(plane_pair[0], plane_pair[1]),
                         (jnp.moveaxis(before, 1, 0), omega))
        relaxed = jnp.moveaxis(planes, 0, 1)
        gathered = []
        for direction in range(27):
            step_x = direction // 9 - 1
            step_y = (direction // 3) % 3 - 1
            step_z = direction % 3 - 1
            pulled = jnp.roll(relaxed[direction], (step_x, step_y, step_z), axis=(0, 1, 2))
            blocked = jnp.roll(solid_cell, (step_x, step_y, step_z), axis=(0, 1, 2))
            bounced = jnp.where(blocked, relaxed[26 - direction], pulled)
            gathered.append(jnp.where(solid_cell, before[direction], bounced))
        read = jnp.stack(gathered)
        current = read / weight
        signal = signal + radiate(read, radiation, bins, counts, sample_site, sample_patch, step_index)
    return current, signal
```

```python
import functools

import jax
import jax.numpy as jnp
from jax import lax
from jax.experimental import pallas as pl
from jax.experimental.pallas import tpu as pltpu
from jax.sharding import PartitionSpec as P

CX = 4
CY = 16
NZ = 256
ZS = 128
SAMP = 16
LEVELS = 128
COLUMN = 128
OWN = 32
WALL = 2.0**100
WALL_TEST = 2.0**60
MESH = pl.DeviceIdType.MESH
F32 = jnp.float32
BF16 = jnp.bfloat16
CORNERS = ((-1, -1), (-1, 1), (1, -1), (1, 1))


def moments(g):
    def pair(lo, hi):
        return lo + hi, hi - lo

    s0 = [[None] * 3 for _ in range(3)]
    s1 = [[None] * 3 for _ in range(3)]
    s2 = [[None] * 3 for _ in range(3)]
    for a in range(3):
        for b in range(3):
            lo, mid, hi = g(a, b, 0), g(a, b, 1), g(a, b, 2)
            s2[a][b], s1[a][b] = pair(lo, hi)
            s0[a][b] = 4.0 * mid + s2[a][b]
    t00, t10, t20, t01, t11, t02 = [], [], [], [], [], []
    for a in range(3):
        ends, gap = pair(s0[a][0], s0[a][2])
        t00.append(4.0 * s0[a][1] + ends)
        t10.append(gap)
        t20.append(ends)
        ends, gap = pair(s1[a][0], s1[a][2])
        t01.append(4.0 * s1[a][1] + ends)
        t11.append(gap)
        t02.append(4.0 * s2[a][1] + (s2[a][0] + s2[a][2]))

    def whole(t):
        return 4.0 * t[1] + (t[0] + t[2])

    m200 = t00[0] + t00[2]
    return {
        "000": 4.0 * t00[1] + m200,
        "100": t00[2] - t00[0],
        "200": m200,
        "010": whole(t10),
        "110": t10[2] - t10[0],
        "020": whole(t20),
        "001": whole(t01),
        "101": t01[2] - t01[0],
        "011": whole(t11),
        "002": whole(t02),
    }


def line(o0, o1, o2, v):
    if o1 is None:
        d = v * o0
        e = o2 + v * d
    else:
        d = o1 + v * o0
        e = o2 + v * (o1 + d)
    return e - d, 0.5 * (o0 - e), e + d


def odd_line(o1, v):
    c = v * o1
    e = c + c
    return e - o1, -c, e + o1


def collided(m, omega):
    inv_m = 1.0 / m["000"]
    ux, uy, uz = m["100"] * inv_m, m["010"] * inv_m, m["001"] * inv_m
    n = {k: 0.125 * v for k, v in m.items()}
    rho, mx, my, mz = n["000"], n["100"], n["010"], n["001"]
    inverse = 8.0 * inv_m
    retain = 1.0 - omega
    c200 = n["200"] - mx * ux
    c020 = n["020"] - my * uy
    c002 = n["002"] - mz * uz
    third = 1.0 / 3.0
    d1 = retain * (c200 - c020)
    d2 = retain * (c200 - c002)
    total = rho + d1 + d2
    kxx = total * third
    kyy = (total - 3.0 * d1) * third
    kzz = (total - 3.0 * d2) * third
    kxy = retain * (n["110"] - mx * uy)
    kxz = retain * (n["101"] - mx * uz)
    kyz = retain * (n["011"] - my * uz)
    sxy, sxz, syz = kxy * kxy, kxz * kxz, kyz * kyz
    xy_xz, xy_yz, xz_yz = kxy * kxz, kxy * kyz, kxz * kyz
    k220 = (kxx * kyy + 2.0 * sxy) * inverse
    k202 = (kxx * kzz + 2.0 * sxz) * inverse
    yy_zz = kyy * kzz
    k022 = (yy_zz + 2.0 * syz) * inverse
    k211 = (kxx * kyz + 2.0 * xy_xz) * inverse
    k121 = (kyy * kxz + 2.0 * xy_yz) * inverse
    k112 = (kzz * kxy + 2.0 * xz_yz) * inverse
    k222 = (
        kxx * (yy_zz + 2.0 * syz) + 2.0 * (kyy * sxz + kzz * sxy) + 8.0 * (kxy * xz_yz)
    ) * (inverse * inverse)
    cols = {
        (0, 0): line(rho, None, kxx, ux),
        (1, 0): odd_line(kxy, ux),
        (2, 0): line(kyy, None, k220, ux),
        (0, 1): odd_line(kxz, ux),
        (1, 1): line(kyz, None, k211, ux),
        (2, 1): odd_line(k121, ux),
        (0, 2): line(kzz, None, k202, ux),
        (1, 2): odd_line(k112, ux),
        (2, 2): line(k022, None, k222, ux),
    }
    for a in range(3):
        by_y = [line(cols[0, c][a], cols[1, c][a], cols[2, c][a], uy) for c in range(3)]
        for b in range(3):
            ends = line(by_y[0][b], by_y[1][b], by_y[2][b], uz)
            for c in range(3):
                yield 9 * a + 3 * b + c, ends[c]


def kernel(
    n_gx,
    n_gy,
    count_ref,
    site_ref,
    patch_ref,
    pop_hbm,
    omega_hbm,
    walls_hbm,
    rad_hbm,
    bins_hbm,
    adv_hbm,
    sig_ref,
    f_ref,
    rel,
    omega,
    walls,
    rad,
    bins,
    xsend,
    xrecv,
    ysend,
    yrecv,
    csend,
    crecv,
    lv_own,
    lv_gy,
    lv_sum,
    lv_in,
    one_hot,
    fields,
    rows,
    resp,
    resp_in,
    load_sem,
    out_sem,
    halo_send,
    halo_recv,
    lvg_send,
    lvg_recv,
    lva_send,
    lva_recv,
    row_send,
    row_recv,
    resp_send,
    resp_recv,
):
    me_x, me_y = lax.axis_index("gx"), lax.axis_index("gy")

    def at_x(d):
        return lax.rem(me_x + (d + n_gx), n_gx)

    def at_y(d):
        return lax.rem(me_y + (d + n_gy), n_gy)

    layers = (0, 3, 1, 2)
    pop_loads = [
        pltpu.make_async_copy(pop_hbm.at[:, x], f_ref.at[:, x], load_sem.at[x]) for x in range(CX)
    ]
    omega_load = pltpu.make_async_copy(omega_hbm, omega, load_sem.at[4])
    walls_load = pltpu.make_async_copy(walls_hbm, walls, load_sem.at[5])
    bins_load = pltpu.make_async_copy(
        bins_hbm.at[pl.ds(pl.multiple_of(me_y * COLUMN, COLUMN), COLUMN)], bins, load_sem.at[6]
    )
    rad_load = pltpu.make_async_copy(rad_hbm.at[:, me_y], rad, load_sem.at[7])
    bins_load.start()
    omega_load.start()
    walls_load.start()
    for x in layers:
        pop_loads[x].start()
    rad_load.start()

    barrier = pltpu.get_barrier_semaphore()

    @pl.loop(1, n_gx)
    def _(d):
        pl.semaphore_signal(barrier, inc=1, device_id=(at_x(d), me_y), device_id_type=MESH)

    for e in range(1, n_gy):
        pl.semaphore_signal(barrier, inc=1, device_id=(me_x, at_y(e)), device_id_type=MESH)
    for sx, sy in CORNERS:
        pl.semaphore_signal(barrier, inc=1, device_id=(at_x(sx), at_y(sy)), device_id_type=MESH)

    lane = lax.broadcasted_iota(jnp.int32, (COLUMN, 128), 1)
    sub = lax.broadcasted_iota(jnp.int32, (COLUMN, 128), 0)
    slot_patch = jnp.full((COLUMN, 128), -1, jnp.int32)
    for k in range(SAMP):
        local = patch_ref[0, k] - me_y * COLUMN
        slot_patch = jnp.where(lane % 64 == me_y * SAMP + k, local, slot_patch)
    pick = (slot_patch == sub).astype(BF16)
    bins_load.wait()
    level = lax.dot_general(
        bins[...].astype(F32).astype(BF16), pick, (((0,), (0,)), ((), ())), preferred_element_type=F32
    )
    lane_b = lax.broadcasted_iota(jnp.int32, (n_gx, 128), 1)
    later = (lane_b >= 64) & ((lane_b % 64) // SAMP == me_y)
    level = level + jnp.where(later, 1.0, 0.0)
    for b in range(n_gx):
        lv_own[b] = level[b : b + 1, :]

    sub_k = lax.broadcasted_iota(jnp.int32, (SAMP, 128), 0)
    lane_k = lax.broadcasted_iota(jnp.int32, (SAMP, 128), 1)
    target = jnp.full((SAMP, 128), -1, jnp.int32)
    for k in range(SAMP):
        site = site_ref[0, k]
        target = jnp.where(sub_k == k, (site % 2) * 64 + site // 2, target)
    live = (target == lane_k) & (sub_k < count_ref[0, 0])
    selector = live.astype(BF16)

    def collide(first, step, with_fields):
        @pl.loop(0, 8)
        def _(j):
            x = first + (j // 4) * step
            y0 = pl.multiple_of(((j // 2) % 2) * 8, 8)
            z0 = pl.multiple_of((j % 2) * 128, 128)

            def g(a, b, c):
                return f_ref[9 * a + 3 * b + c, x, pl.ds(y0, 8), pl.ds(z0, 128)]

            m = moments(g)
            solid = walls[x, pl.ds(y0, 8), pl.ds(z0, 128)] == 1
            if with_fields:
                put_fields(m, x, y0, j % 2)
            for i, value in collided(m, omega[x, pl.ds(y0, 8), pl.ds(z0, 128)]):
                rel[i, x + 1, pl.ds(y0 + 8, 8), pl.ds(z0, 128)] = jnp.where(solid, WALL, value)

    def put_fields(m, x, y0, half):
        row = pl.multiple_of(half * 64 + x * CY + y0, 8)
        scale = 1.0 / 216.0
        fields[0, pl.ds(row, 8), :] = m["000"] * scale - 1.0
        fields[1, pl.ds(row, 8), :] = m["100"] * scale
        fields[2, pl.ds(row, 8), :] = m["010"] * scale
        fields[3, pl.ds(row, 8), :] = m["001"] * scale

    def x_copy(s, side):
        sx = 2 * side - 1
        return pltpu.make_async_remote_copy(
            src_ref=xsend.at[s, side],
            dst_ref=xrecv.at[s, side],
            send_sem=halo_send.at[s, side],
            recv_sem=halo_recv.at[s, side],
            device_id=(at_x(sx), me_y),
            device_id_type=MESH,
        )

    def y_copy(s, side):
        sy = 2 * side - 1
        return pltpu.make_async_remote_copy(
            src_ref=ysend.at[s, side],
            dst_ref=yrecv.at[s, side],
            send_sem=halo_send.at[s, 2 + side],
            recv_sem=halo_recv.at[s, 2 + side],
            device_id=(me_x, at_y(sy)),
            device_id_type=MESH,
        )

    def c_copy(s, corner):
        sx, sy = CORNERS[corner]
        return pltpu.make_async_remote_copy(
            src_ref=csend.at[s, corner],
            dst_ref=crecv.at[s, corner],
            send_sem=halo_send.at[s, 4 + corner],
            recv_sem=halo_recv.at[s, 4 + corner],
            device_id=(at_x(sx), at_y(sy)),
            device_id_type=MESH,
        )

    def crossing(sy):
        return [9 * a + 3 * (sy + 1) + c for a in range(3) for c in range(3)]

    def send_x(s):
        for side in range(2):
            for j in range(9):
                value = rel[18 * side + j, 1 + 3 * side, pl.ds(8, CY), :]
                xsend[s, side, j] = (value - 1.0).astype(BF16)
            x_copy(s, side).start()

    def send_y(s):
        for side in range(2):
            edge = 8 + 15 * side
            for j, i in enumerate(crossing(2 * side - 1)):
                for x in range(CX):
                    ysend[s, side, 4 * j + x : 4 * j + x + 1, :] = rel[i, x + 1, edge : edge + 1, :]
            y_copy(s, side).start()
        for corner, (sx, sy) in enumerate(CORNERS):
            edge = 23 if sy > 0 else 8
            x = 4 if sx > 0 else 1
            for c in range(3):
                i = 9 * (sx + 1) + 3 * (sy + 1) + c
                csend[s, corner, c : c + 1, :] = rel[i, x, edge : edge + 1, :]
            c_copy(s, corner).start()

    def take_halo(s):
        for side in range(2):
            y_copy(s, side).wait()
            edge = 7 if side == 1 else 24
            for j, i in enumerate(crossing(2 * side - 1)):
                for x in range(CX):
                    rel[i, x + 1, edge : edge + 1, :] = yrecv[s, side, 4 * j + x : 4 * j + x + 1, :]
        for corner, (sx, sy) in enumerate(CORNERS):
            c_copy(s, corner).wait()
            edge = 7 if sy > 0 else 24
            x = 0 if sx > 0 else 5
            for c in range(3):
                i = 9 * (sx + 1) + 3 * (sy + 1) + c
                rel[i, x, edge : edge + 1, :] = crecv[s, corner, c : c + 1, :]
        for side in range(2):
            x_copy(s, side).wait()
            for j in range(9):
                rel[18 * side + j, 5 - 5 * side, pl.ds(8, CY), :] = (
                    xrecv[s, side, j].astype(F32) + 1.0
                )

    def stream():
        @pl.loop(0, CX)
        def _(x):
            solid = walls[x] == 1
            for i in range(27):
                cx, cy, cz = i // 9 - 1, (i // 3) % 3 - 1, i % 3 - 1
                source = rel[i, x + 1 - cx, pl.ds(8 - cy, CY), :]
                if cz:
                    source = pltpu.roll(source, cz % NZ, 1)
                bounced = jnp.where(
                    source > WALL_TEST, rel[26 - i, x + 1, pl.ds(8, CY), :], source
                )
                f_ref[i, x] = jnp.where(solid, f_ref[i, x], bounced)

    def send_rows(s):
        for part in range(4):
            taken = jnp.dot(selector, fields[part].astype(BF16), preferred_element_type=F32)
            rows[s, me_y, :, part * ZS : (part + 1) * ZS] = taken.astype(BF16)
        for e in range(1, n_gy):
            row_copy(s, e).start()

    def row_copy(s, e):
        return pltpu.make_async_remote_copy(
            src_ref=rows.at[s, me_y],
            dst_ref=rows.at[s, me_y],
            send_sem=row_send.at[s, e],
            recv_sem=row_recv.at[s, e],
            device_id=(me_x, at_y(e)),
            device_id_type=MESH,
        )

    def take_rows(s):
        for e in range(1, n_gy):
            pltpu.make_async_remote_copy(
                src_ref=rows.at[s, me_y],
                dst_ref=rows.at[s, at_y(-e)],
                send_sem=row_send.at[s, e],
                recv_sem=row_recv.at[s, e],
                device_id=(me_x, at_y(e)),
                device_id_type=MESH,
            ).wait()

    def lvg_copy(e):
        return pltpu.make_async_remote_copy(
            src_ref=lv_own,
            dst_ref=lv_gy.at[e],
            send_sem=lvg_send.at[e],
            recv_sem=lvg_recv.at[e],
            device_id=(me_x, at_y(e)),
            device_id_type=MESH,
        )

    def lva_copy(d):
        return pltpu.make_async_remote_copy(
            src_ref=lv_sum.at[at_x(d)],
            dst_ref=lv_in.at[d],
            send_sem=lva_send.at[d],
            recv_sem=lva_recv.at[d],
            device_id=(at_x(d), me_y),
            device_id_type=MESH,
        )

    def resp_copy(d):
        return pltpu.make_async_remote_copy(
            src_ref=resp.at[at_x(d)],
            dst_ref=resp_in.at[d],
            send_sem=resp_send.at[d],
            recv_sem=resp_recv.at[d],
            device_id=(at_x(d), me_y),
            device_id_type=MESH,
        )

    omega_load.wait()
    walls_load.wait()
    pop_loads[0].wait()
    pop_loads[3].wait()
    collide(0, 3, False)
    pl.semaphore_wait(barrier, n_gx - 1 + n_gy - 1 + 4)
    send_x(0)
    for e in range(1, n_gy):
        lvg_copy(e).start()
    pop_loads[1].wait()
    pop_loads[2].wait()
    collide(1, 1, False)
    send_y(0)

    summed = lv_own[...]
    for e in range(1, n_gy):
        lvg_copy(e).wait()
        summed = summed + lv_gy[e]
    lv_sum[...] = summed

    @pl.loop(1, n_gx)
    def _(d):
        lva_copy(d).start()

    lv_in[0] = lv_sum[me_x]
    take_halo(0)
    stream()

    collide(0, 3, True)
    send_x(1)
    collide(1, 1, True)
    send_y(1)
    send_rows(0)

    @pl.loop(0, n_gx)
    def _(d):
        @pl.when(d > 0)
        def _():
            lva_copy(d).wait()

        wanted = lax.broadcasted_iota(jnp.int32, (LEVELS, 128), 0).astype(F32)
        one_hot[d] = (jnp.broadcast_to(lv_in[d], (LEVELS, 128)) == wanted).astype(BF16)

    take_rows(0)
    rad_load.wait()
    take_halo(1)
    stream()
    out_copy = pltpu.make_async_copy(f_ref, adv_hbm, out_sem)
    out_copy.start()

    @pl.loop(0, 16)
    def _(j):
        x = j // 4
        y0 = pl.multiple_of(((j // 2) % 2) * 8, 8)
        z0 = pl.multiple_of((j % 2) * 128, 128)

        def g(a, b, c):
            return f_ref[9 * a + 3 * b + c, x, pl.ds(y0, 8), pl.ds(z0, 128)]

        put_fields(moments(g), x, y0, j % 2)

    send_rows(1)
    take_rows(1)
    all_rows = rows[...].reshape(2 * n_gy * SAMP, 4 * ZS)

    @pl.loop(0, n_gx // 4)
    def _(t):
        block = rad[pl.ds(t * 4, 4)].reshape(4 * OWN, 4 * ZS)
        seen = lax.dot_general(block, all_rows, (((1,), (1,)), ((), ())), preferred_element_type=F32)
        resp[pl.ds(t * 4, 4)] = seen.astype(BF16).reshape(4, OWN, 128)

    @pl.loop(1, n_gx)
    def _(d):
        resp_copy(d).start()

    resp_in[0] = resp[me_x]

    def add(d, total):
        @pl.when(d > 0)
        def _():
            resp_copy(d).wait()

        return total + lax.dot_general(
            resp_in[d], one_hot[d], (((1,), (1,)), ((), ())), preferred_element_type=F32
        )

    sig_ref[...] = lax.fori_loop(0, n_gx, add, jnp.zeros((OWN, LEVELS), F32))
    out_copy.wait()


def per_device(populations, omega, walls, radiation, bins, counts, sample_site, sample_patch):
    n_gx, n_gy = lax.axis_size("gx"), lax.axis_size("gy")
    hbm = pl.BlockSpec(memory_space=pl.ANY)
    smem = pl.BlockSpec(memory_space=pltpu.SMEM)
    vmem = pl.BlockSpec(memory_space=pltpu.VMEM)
    dma = pltpu.SemaphoreType.DMA
    scratch = [
        pltpu.VMEM((27, CX, CY, NZ), F32),
        pltpu.VMEM((27, CX + 2, CY + 16, NZ), F32),
        pltpu.VMEM((CX, CY, NZ), F32),
        pltpu.VMEM((CX, CY, NZ), jnp.int32),
        pltpu.VMEM((n_gx, OWN, 4 * ZS), BF16),
        pltpu.VMEM((COLUMN, n_gx), jnp.int32),
        pltpu.VMEM((2, 2, 9, CY, NZ), BF16),
        pltpu.VMEM((2, 2, 9, CY, NZ), BF16),
        pltpu.VMEM((2, 2, 40, NZ), F32),
        pltpu.VMEM((2, 2, 40, NZ), F32),
        pltpu.VMEM((2, 4, 8, NZ), F32),
        pltpu.VMEM((2, 4, 8, NZ), F32),
        pltpu.VMEM((n_gx, 1, 128), F32),
        pltpu.VMEM((n_gy, n_gx, 1, 128), F32),
        pltpu.VMEM((n_gx, 1, 128), F32),
        pltpu.VMEM((n_gx, 1, 128), F32),
        pltpu.VMEM((n_gx, LEVELS, 128), BF16),
        pltpu.VMEM((4, 128, ZS), F32),
        pltpu.VMEM((2, n_gy, SAMP, 4 * ZS), BF16),
        pltpu.VMEM((n_gx, OWN, 128), BF16),
        pltpu.VMEM((n_gx, OWN, 128), BF16),
        dma((8,)),
        dma,
        dma((2, 8)),
        dma((2, 8)),
        dma((n_gy,)),
        dma((n_gy,)),
        dma((n_gx,)),
        dma((n_gx,)),
        dma((2, n_gy)),
        dma((2, n_gy)),
        dma((n_gx,)),
        dma((n_gx,)),
    ]
    return pl.pallas_call(
        functools.partial(kernel, n_gx, n_gy),
        out_shape=(
            jax.ShapeDtypeStruct((27, CX, CY, NZ), F32),
            jax.ShapeDtypeStruct((OWN, LEVELS), F32),
        ),
        in_specs=[smem] * 3 + [hbm] * 5,
        out_specs=(hbm, vmem),
        scratch_shapes=scratch,
        compiler_params=pltpu.CompilerParams(collective_id=0, has_side_effects=True),
        name="lattice_far_field",
    )(
        counts,
        sample_site.reshape(1, SAMP),
        sample_patch.reshape(1, SAMP),
        populations,
        omega,
        walls,
        radiation.reshape(n_gx, n_gy, OWN, 4 * ZS),
        bins,
    )


def solution(mesh):
    return jax.shard_map(
        per_device,
        mesh=mesh,
        in_specs=(
            P(None, "gx", "gy", None),
            P("gx", "gy", None),
            P("gx", "gy", None),
            P(),
            P(),
            P("gx", "gy"),
            P("gx", "gy", None),
            P("gx", "gy", None),
        ),
        out_specs=(P(None, "gx", "gy", None), P(("gx", "gy"), None)),
        check_vma=False,
    )
```

```python
import functools

import jax
import jax.numpy as jnp
from jax import lax
from jax.experimental import pallas as pl
from jax.experimental.pallas import tpu as pltpu
from jax.sharding import PartitionSpec as P

CX = 4
CY = 16
NZ = 256
ZS = 128
SAMP = 16
LEVELS = 128
COLUMN = 128
OWN = 32
WALL = 2.0**100
WALL_TEST = 2.0**60
MESH = pl.DeviceIdType.MESH
F32 = jnp.float32
BF16 = jnp.bfloat16
CORNERS = ((-1, -1), (-1, 1), (1, -1), (1, 1))


def moments(g):
    def pair(lo, hi):
        return lo + hi, hi - lo

    s0 = [[None] * 3 for _ in range(3)]
    s1 = [[None] * 3 for _ in range(3)]
    s2 = [[None] * 3 for _ in range(3)]
    for a in range(3):
        for b in range(3):
            lo, mid, hi = g(a, b, 0), g(a, b, 1), g(a, b, 2)
            s2[a][b], s1[a][b] = pair(lo, hi)
            s0[a][b] = 4.0 * mid + s2[a][b]
    t00, t10, t20, t01, t11, t02 = [], [], [], [], [], []
    for a in range(3):
        ends, gap = pair(s0[a][0], s0[a][2])
        t00.append(4.0 * s0[a][1] + ends)
        t10.append(gap)
        t20.append(ends)
        ends, gap = pair(s1[a][0], s1[a][2])
        t01.append(4.0 * s1[a][1] + ends)
        t11.append(gap)
        t02.append(4.0 * s2[a][1] + (s2[a][0] + s2[a][2]))

    def whole(t):
        return 4.0 * t[1] + (t[0] + t[2])

    m200 = t00[0] + t00[2]
    return {
        "000": 4.0 * t00[1] + m200,
        "100": t00[2] - t00[0],
        "200": m200,
        "010": whole(t10),
        "110": t10[2] - t10[0],
        "020": whole(t20),
        "001": whole(t01),
        "101": t01[2] - t01[0],
        "011": whole(t11),
        "002": whole(t02),
    }


def line(o0, o1, o2, v):
    if o1 is None:
        d = v * o0
        e = o2 + v * d
    else:
        d = o1 + v * o0
        e = o2 + v * (o1 + d)
    return e - d, 0.5 * (o0 - e), e + d


def odd_line(o1, v):
    c = v * o1
    e = c + c
    return e - o1, -c, e + o1


def collided(m, omega):
    inv_m = 1.0 / m["000"]
    ux, uy, uz = m["100"] * inv_m, m["010"] * inv_m, m["001"] * inv_m
    n = {k: 0.125 * v for k, v in m.items()}
    rho, mx, my, mz = n["000"], n["100"], n["010"], n["001"]
    inverse = 8.0 * inv_m
    retain = 1.0 - omega
    c200 = n["200"] - mx * ux
    c020 = n["020"] - my * uy
    c002 = n["002"] - mz * uz
    third = 1.0 / 3.0
    d1 = retain * (c200 - c020)
    d2 = retain * (c200 - c002)
    total = rho + d1 + d2
    kxx = total * third
    kyy = (total - 3.0 * d1) * third
    kzz = (total - 3.0 * d2) * third
    kxy = retain * (n["110"] - mx * uy)
    kxz = retain * (n["101"] - mx * uz)
    kyz = retain * (n["011"] - my * uz)
    sxy, sxz, syz = kxy * kxy, kxz * kxz, kyz * kyz
    xy_xz, xy_yz, xz_yz = kxy * kxz, kxy * kyz, kxz * kyz
    k220 = (kxx * kyy + 2.0 * sxy) * inverse
    k202 = (kxx * kzz + 2.0 * sxz) * inverse
    yy_zz = kyy * kzz
    k022 = (yy_zz + 2.0 * syz) * inverse
    k211 = (kxx * kyz + 2.0 * xy_xz) * inverse
    k121 = (kyy * kxz + 2.0 * xy_yz) * inverse
    k112 = (kzz * kxy + 2.0 * xz_yz) * inverse
    k222 = (
        kxx * (yy_zz + 2.0 * syz) + 2.0 * (kyy * sxz + kzz * sxy) + 8.0 * (kxy * xz_yz)
    ) * (inverse * inverse)
    cols = {
        (0, 0): line(rho, None, kxx, ux),
        (1, 0): odd_line(kxy, ux),
        (2, 0): line(kyy, None, k220, ux),
        (0, 1): odd_line(kxz, ux),
        (1, 1): line(kyz, None, k211, ux),
        (2, 1): odd_line(k121, ux),
        (0, 2): line(kzz, None, k202, ux),
        (1, 2): odd_line(k112, ux),
        (2, 2): line(k022, None, k222, ux),
    }
    for a in range(3):
        by_y = [line(cols[0, c][a], cols[1, c][a], cols[2, c][a], uy) for c in range(3)]
        for b in range(3):
            ends = line(by_y[0][b], by_y[1][b], by_y[2][b], uz)
            for c in range(3):
                yield 9 * a + 3 * b + c, ends[c]


def kernel(
    n_gx,
    n_gy,
    count_ref,
    site_ref,
    patch_ref,
    pop_hbm,
    omega_hbm,
    walls_hbm,
    rad_hbm,
    bins_hbm,
    adv_ref,
    sig_ref,
    f_ref,
    rel,
    omega,
    walls,
    rad,
    bins,
    xsend,
    xrecv,
    ysend,
    yrecv,
    csend,
    crecv,
    lv_own,
    lv_gy,
    lv_sum,
    lv_in,
    one_hot,
    fields,
    rows,
    resp,
    resp_in,
    load_sem,
    halo_send,
    halo_recv,
    lvg_send,
    lvg_recv,
    lva_send,
    lva_recv,
    row_send,
    row_recv,
    resp_send,
    resp_recv,
):
    me_x, me_y = lax.axis_index("gx"), lax.axis_index("gy")

    def at_x(d):
        return lax.rem(me_x + (d + n_gx), n_gx)

    def at_y(d):
        return lax.rem(me_y + (d + n_gy), n_gy)

    layers = (0, 3, 1, 2)
    pop_loads = [
        pltpu.make_async_copy(pop_hbm.at[:, x], f_ref.at[:, x], load_sem.at[x]) for x in range(CX)
    ]
    omega_load = pltpu.make_async_copy(omega_hbm, omega, load_sem.at[4])
    walls_load = pltpu.make_async_copy(walls_hbm, walls, load_sem.at[5])
    bins_load = pltpu.make_async_copy(
        bins_hbm.at[:, pl.ds(pl.multiple_of(me_y * COLUMN, COLUMN), COLUMN)], bins, load_sem.at[6]
    )
    rad_load = pltpu.make_async_copy(rad_hbm.at[:, me_y], rad, load_sem.at[7])
    bins_load.start()
    omega_load.start()
    walls_load.start()
    for x in layers:
        pop_loads[x].start()
    rad_load.start()

    barrier = pltpu.get_barrier_semaphore()

    @pl.loop(1, n_gx)
    def _(d):
        pl.semaphore_signal(barrier, inc=1, device_id=(at_x(d), me_y), device_id_type=MESH)

    for e in range(1, n_gy):
        pl.semaphore_signal(barrier, inc=1, device_id=(me_x, at_y(e)), device_id_type=MESH)
    for sx, sy in CORNERS:
        pl.semaphore_signal(barrier, inc=1, device_id=(at_x(sx), at_y(sy)), device_id_type=MESH)

    def collide(first, step, with_fields):
        @pl.loop(0, 8)
        def _(j):
            x = first + (j // 4) * step
            y0 = pl.multiple_of(((j // 2) % 2) * 8, 8)
            z0 = pl.multiple_of((j % 2) * 128, 128)

            def g(a, b, c):
                return f_ref[9 * a + 3 * b + c, x, pl.ds(y0, 8), pl.ds(z0, 128)]

            m = moments(g)
            solid = walls[x, pl.ds(y0, 8), pl.ds(z0, 128)] == 1
            if with_fields:
                put_fields(m, x, y0, j % 2)
            for i, value in collided(m, omega[x, pl.ds(y0, 8), pl.ds(z0, 128)]):
                rel[i, x + 1, pl.ds(y0 + 8, 8), pl.ds(z0, 128)] = jnp.where(solid, WALL, value)

    def put_fields(m, x, y0, half):
        row = pl.multiple_of(half * 64 + x * CY + y0, 8)
        scale = 1.0 / 216.0
        fields[0, pl.ds(row, 8), :] = m["000"] * scale - 1.0
        fields[1, pl.ds(row, 8), :] = m["100"] * scale
        fields[2, pl.ds(row, 8), :] = m["010"] * scale
        fields[3, pl.ds(row, 8), :] = m["001"] * scale

    def x_copy(s, side):
        sx = 2 * side - 1
        return pltpu.make_async_remote_copy(
            src_ref=xsend.at[s, side],
            dst_ref=xrecv.at[s, side],
            send_sem=halo_send.at[s, side],
            recv_sem=halo_recv.at[s, side],
            device_id=(at_x(sx), me_y),
            device_id_type=MESH,
        )

    def y_copy(s, side):
        sy = 2 * side - 1
        return pltpu.make_async_remote_copy(
            src_ref=ysend.at[s, side],
            dst_ref=yrecv.at[s, side],
            send_sem=halo_send.at[s, 2 + side],
            recv_sem=halo_recv.at[s, 2 + side],
            device_id=(me_x, at_y(sy)),
            device_id_type=MESH,
        )

    def c_copy(s, corner):
        sx, sy = CORNERS[corner]
        return pltpu.make_async_remote_copy(
            src_ref=csend.at[s, corner],
            dst_ref=crecv.at[s, corner],
            send_sem=halo_send.at[s, 4 + corner],
            recv_sem=halo_recv.at[s, 4 + corner],
            device_id=(at_x(sx), at_y(sy)),
            device_id_type=MESH,
        )

    def crossing(sy):
        return [9 * a + 3 * (sy + 1) + c for a in range(3) for c in range(3)]

    def send_x(s):
        for side in range(2):
            for j in range(9):
                value = rel[18 * side + j, 1 + 3 * side, pl.ds(8, CY), :]
                xsend[s, side, j] = (value - 1.0).astype(BF16)
            x_copy(s, side).start()

    def send_y(s):
        for side in range(2):
            edge = 8 + 15 * side
            for j, i in enumerate(crossing(2 * side - 1)):
                for x in range(CX):
                    ysend[s, side, 4 * j + x : 4 * j + x + 1, :] = rel[i, x + 1, edge : edge + 1, :]
            y_copy(s, side).start()
        for corner, (sx, sy) in enumerate(CORNERS):
            edge = 23 if sy > 0 else 8
            x = 4 if sx > 0 else 1
            for c in range(3):
                i = 9 * (sx + 1) + 3 * (sy + 1) + c
                csend[s, corner, c : c + 1, :] = rel[i, x, edge : edge + 1, :]
            c_copy(s, corner).start()

    def take_halo(s):
        for side in range(2):
            y_copy(s, side).wait()
            edge = 7 if side == 1 else 24
            for j, i in enumerate(crossing(2 * side - 1)):
                for x in range(CX):
                    rel[i, x + 1, edge : edge + 1, :] = yrecv[s, side, 4 * j + x : 4 * j + x + 1, :]
        for corner, (sx, sy) in enumerate(CORNERS):
            c_copy(s, corner).wait()
            edge = 7 if sy > 0 else 24
            x = 0 if sx > 0 else 5
            for c in range(3):
                i = 9 * (sx + 1) + 3 * (sy + 1) + c
                rel[i, x, edge : edge + 1, :] = crecv[s, corner, c : c + 1, :]
        for side in range(2):
            x_copy(s, side).wait()
            for j in range(9):
                rel[18 * side + j, 5 - 5 * side, pl.ds(8, CY), :] = (
                    xrecv[s, side, j].astype(F32) + 1.0
                )

    def stream(to_ref):
        @pl.loop(0, CX)
        def _(x):
            solid = walls[x] == 1
            for i in range(27):
                cx, cy, cz = i // 9 - 1, (i // 3) % 3 - 1, i % 3 - 1
                source = rel[i, x + 1 - cx, pl.ds(8 - cy, CY), :]
                if cz:
                    source = pltpu.roll(source, cz % NZ, 1)
                bounced = jnp.where(
                    source > WALL_TEST, rel[26 - i, x + 1, pl.ds(8, CY), :], source
                )
                to_ref[i, x] = jnp.where(solid, f_ref[i, x], bounced)

    def send_rows(s):
        for part in range(4):
            taken = jnp.dot(selector, fields[part].astype(BF16), preferred_element_type=F32)
            rows[s, me_y, :, part * ZS : (part + 1) * ZS] = taken.astype(BF16)
        for e in range(1, n_gy):
            row_copy(s, e).start()

    def row_copy(s, e):
        return pltpu.make_async_remote_copy(
            src_ref=rows.at[s, me_y],
            dst_ref=rows.at[s, me_y],
            send_sem=row_send.at[s, e],
            recv_sem=row_recv.at[s, e],
            device_id=(me_x, at_y(e)),
            device_id_type=MESH,
        )

    def take_rows(s):
        for e in range(1, n_gy):
            pltpu.make_async_remote_copy(
                src_ref=rows.at[s, me_y],
                dst_ref=rows.at[s, at_y(-e)],
                send_sem=row_send.at[s, e],
                recv_sem=row_recv.at[s, e],
                device_id=(me_x, at_y(e)),
                device_id_type=MESH,
            ).wait()

    def lvg_copy(e):
        return pltpu.make_async_remote_copy(
            src_ref=lv_own,
            dst_ref=lv_gy.at[e],
            send_sem=lvg_send.at[e],
            recv_sem=lvg_recv.at[e],
            device_id=(me_x, at_y(e)),
            device_id_type=MESH,
        )

    def lva_copy(d):
        return pltpu.make_async_remote_copy(
            src_ref=lv_sum.at[at_x(d)],
            dst_ref=lv_in.at[d],
            send_sem=lva_send.at[d],
            recv_sem=lva_recv.at[d],
            device_id=(at_x(d), me_y),
            device_id_type=MESH,
        )

    def resp_copy(d):
        return pltpu.make_async_remote_copy(
            src_ref=resp.at[at_x(d)],
            dst_ref=resp_in.at[d],
            send_sem=resp_send.at[d],
            recv_sem=resp_recv.at[d],
            device_id=(at_x(d), me_y),
            device_id_type=MESH,
        )

    omega_load.wait()
    walls_load.wait()
    pop_loads[0].wait()
    pop_loads[3].wait()
    collide(0, 3, False)
    pl.semaphore_wait(barrier, n_gx - 1 + n_gy - 1 + 4)
    send_x(0)
    pop_loads[1].wait()
    pop_loads[2].wait()
    collide(1, 1, False)
    send_y(0)

    lane = lax.broadcasted_iota(jnp.int32, (COLUMN, 128), 1)
    sub = lax.broadcasted_iota(jnp.int32, (COLUMN, 128), 0)
    slot_patch = jnp.full((COLUMN, 128), -1, jnp.int32)
    for k in range(SAMP):
        local = patch_ref[0, k] - me_y * COLUMN
        slot_patch = jnp.where(lane % 64 == me_y * SAMP + k, local, slot_patch)
    pick = (slot_patch == sub).astype(BF16)
    bins_load.wait()
    level = lax.dot_general(
        bins[...].astype(F32).astype(BF16), pick, (((1,), (0,)), ((), ())), preferred_element_type=F32
    )
    lane_b = lax.broadcasted_iota(jnp.int32, (n_gx, 128), 1)
    later = (lane_b >= 64) & ((lane_b % 64) // SAMP == me_y)
    level = level + jnp.where(later, 1.0, 0.0)
    for b in range(n_gx):
        lv_own[b] = level[b : b + 1, :]
    for e in range(1, n_gy):
        lvg_copy(e).start()

    sub_k = lax.broadcasted_iota(jnp.int32, (SAMP, 128), 0)
    lane_k = lax.broadcasted_iota(jnp.int32, (SAMP, 128), 1)
    target = jnp.full((SAMP, 128), -1, jnp.int32)
    for k in range(SAMP):
        site = site_ref[0, k]
        target = jnp.where(sub_k == k, (site % 2) * 64 + site // 2, target)
    live = (target == lane_k) & (sub_k < count_ref[0, 0])
    selector = live.astype(BF16)

    summed = lv_own[...]
    for e in range(1, n_gy):
        lvg_copy(e).wait()
        summed = summed + lv_gy[e]
    lv_sum[...] = summed

    @pl.loop(1, n_gx)
    def _(d):
        lva_copy(d).start()

    lv_in[0] = lv_sum[me_x]
    take_halo(0)
    stream(f_ref)

    collide(0, 3, True)
    send_x(1)
    collide(1, 1, True)
    send_y(1)
    send_rows(0)

    @pl.loop(0, n_gx)
    def _(d):
        @pl.when(d > 0)
        def _():
            lva_copy(d).wait()

        wanted = lax.broadcasted_iota(jnp.int32, (LEVELS, 128), 0).astype(F32)
        one_hot[d] = (jnp.broadcast_to(lv_in[d], (LEVELS, 128)) == wanted).astype(BF16)

    take_rows(0)
    rad_load.wait()
    take_halo(1)
    stream(adv_ref)

    @pl.loop(0, 16)
    def _(j):
        x = j // 4
        y0 = pl.multiple_of(((j // 2) % 2) * 8, 8)
        z0 = pl.multiple_of((j % 2) * 128, 128)

        def g(a, b, c):
            return adv_ref[9 * a + 3 * b + c, x, pl.ds(y0, 8), pl.ds(z0, 128)]

        put_fields(moments(g), x, y0, j % 2)

    send_rows(1)
    take_rows(1)
    all_rows = rows[...].reshape(2 * n_gy * SAMP, 4 * ZS)

    seen = lax.dot_general(
        rad[...].reshape(n_gx * OWN, 4 * ZS),
        all_rows,
        (((1,), (1,)), ((), ())),
        preferred_element_type=F32,
    )
    resp[...] = seen.astype(BF16).reshape(n_gx, OWN, 128)

    @pl.loop(1, n_gx)
    def _(d):
        resp_copy(d).start()

    resp_in[0] = resp[me_x]
    total = jnp.zeros((OWN, LEVELS), F32)
    per = max(n_gx // 4, 1)
    for start in range(0, n_gx, per):
        group = range(start, start + per)
        for d in group:
            if d > 0:
                resp_copy(d).wait()
        total = total + lax.dot_general(
            jnp.concatenate([resp_in[d] for d in group], axis=1),
            jnp.concatenate([one_hot[d] for d in group], axis=1),
            (((1,), (1,)), ((), ())),
            preferred_element_type=F32,
        )
    sig_ref[...] = total


def finish(adv_in, sig_in, adv_out, sig_out, sem):
    copies = [
        pltpu.make_async_copy(adv_in.at[pl.ds(9 * a, 9)], adv_out.at[pl.ds(9 * a, 9)], sem.at[a])
        for a in range(3)
    ]
    copies.append(pltpu.make_async_copy(sig_in, sig_out, sem.at[3]))
    for copy in copies:
        copy.start()
    for copy in copies:
        copy.wait()


def per_device(populations, omega, walls, radiation, bins, counts, sample_site, sample_patch):
    n_gx, n_gy = lax.axis_size("gx"), lax.axis_size("gy")
    hbm = pl.BlockSpec(memory_space=pl.ANY)
    smem = pl.BlockSpec(memory_space=pltpu.SMEM)
    vmem = pl.BlockSpec(memory_space=pltpu.VMEM)
    dma = pltpu.SemaphoreType.DMA
    scratch = [
        pltpu.VMEM((27, CX, CY, NZ), F32),
        pltpu.VMEM((27, CX + 2, CY + 16, NZ), F32),
        pltpu.VMEM((CX, CY, NZ), F32),
        pltpu.VMEM((CX, CY, NZ), jnp.int32),
        pltpu.VMEM((n_gx, OWN, 4 * ZS), BF16),
        pltpu.VMEM((n_gx, COLUMN), jnp.int32),
        pltpu.VMEM((2, 2, 9, CY, NZ), BF16),
        pltpu.VMEM((2, 2, 9, CY, NZ), BF16),
        pltpu.VMEM((2, 2, 40, NZ), F32),
        pltpu.VMEM((2, 2, 40, NZ), F32),
        pltpu.VMEM((2, 4, 8, NZ), F32),
        pltpu.VMEM((2, 4, 8, NZ), F32),
        pltpu.VMEM((n_gx, 1, 128), F32),
        pltpu.VMEM((n_gy, n_gx, 1, 128), F32),
        pltpu.VMEM((n_gx, 1, 128), F32),
        pltpu.VMEM((n_gx, 1, 128), F32),
        pltpu.VMEM((n_gx, LEVELS, 128), BF16),
        pltpu.VMEM((4, 128, ZS), F32),
        pltpu.VMEM((2, n_gy, SAMP, 4 * ZS), BF16),
        pltpu.VMEM((n_gx, OWN, 128), BF16),
        pltpu.VMEM((n_gx, OWN, 128), BF16),
        dma((8,)),
        dma((2, 8)),
        dma((2, 8)),
        dma((n_gy,)),
        dma((n_gy,)),
        dma((n_gx,)),
        dma((n_gx,)),
        dma((2, n_gy)),
        dma((2, n_gy)),
        dma((n_gx,)),
        dma((n_gx,)),
    ]
    operands = (
        sample_site.reshape(1, SAMP),
        sample_patch.reshape(1, SAMP),
        populations,
        omega,
        walls,
        radiation.reshape(n_gx, n_gy, OWN, 4 * ZS),
        bins.T,
    )
    advanced, signal = pl.pallas_call(
        functools.partial(kernel, n_gx, n_gy),
        out_shape=(
            jax.ShapeDtypeStruct((27, CX, CY, NZ), F32),
            jax.ShapeDtypeStruct((OWN, LEVELS), F32),
        ),
        in_specs=[smem] * 3 + [hbm] * 5,
        out_specs=(vmem, vmem),
        scratch_shapes=scratch,
        compiler_params=pltpu.CompilerParams(
            collective_id=0, has_side_effects=True, vmem_limit_bytes=44 * 2**20
        ),
        name="lattice_far_field",
    )(counts, *[pltpu.with_memory_space_constraint(x, pltpu.HBM) for x in operands])
    return pl.pallas_call(
        finish,
        out_shape=(
            jax.ShapeDtypeStruct((27, CX, CY, NZ), F32),
            jax.ShapeDtypeStruct((OWN, LEVELS), F32),
        ),
        in_specs=[hbm] * 2,
        out_specs=(hbm, hbm),
        scratch_shapes=[dma((4,))],
        compiler_params=pltpu.CompilerParams(vmem_limit_bytes=2**20),
        name="write_out",
    )(advanced, signal)


def solution(mesh):
    return jax.shard_map(
        per_device,
        mesh=mesh,
        in_specs=(
            P(None, "gx", "gy", None),
            P("gx", "gy", None),
            P("gx", "gy", None),
            P(),
            P(),
            P("gx", "gy"),
            P("gx", "gy", None),
            P("gx", "gy", None),
        ),
        out_specs=(P(None, "gx", "gy", None), P(("gx", "gy"), None)),
        check_vma=False,
    )
```

```python
import functools

import jax
import jax.numpy as jnp
from jax import lax
from jax.experimental import pallas as pl
from jax.experimental.pallas import tpu as pltpu
from jax.sharding import PartitionSpec as P

CX = 4
CY = 16
NZ = 256
ZS = 128
SAMP = 16
LEVELS = 128
COLUMN = 128
OWN = 32
WALL = 2.0**100
WALL_TEST = 2.0**60
MESH = pl.DeviceIdType.MESH
F32 = jnp.float32
BF16 = jnp.bfloat16
CORNERS = ((-1, -1), (-1, 1), (1, -1), (1, 1))


def moments(g):
    def pair(lo, hi):
        return lo + hi, hi - lo

    s0 = [[None] * 3 for _ in range(3)]
    s1 = [[None] * 3 for _ in range(3)]
    s2 = [[None] * 3 for _ in range(3)]
    for a in range(3):
        for b in range(3):
            lo, mid, hi = g(a, b, 0), g(a, b, 1), g(a, b, 2)
            s2[a][b], s1[a][b] = pair(lo, hi)
            s0[a][b] = 4.0 * mid + s2[a][b]
    t00, t10, t20, t01, t11, t02 = [], [], [], [], [], []
    for a in range(3):
        ends, gap = pair(s0[a][0], s0[a][2])
        t00.append(4.0 * s0[a][1] + ends)
        t10.append(gap)
        t20.append(ends)
        ends, gap = pair(s1[a][0], s1[a][2])
        t01.append(4.0 * s1[a][1] + ends)
        t11.append(gap)
        t02.append(4.0 * s2[a][1] + (s2[a][0] + s2[a][2]))

    def whole(t):
        return 4.0 * t[1] + (t[0] + t[2])

    m200 = t00[0] + t00[2]
    return {
        "000": 4.0 * t00[1] + m200,
        "100": t00[2] - t00[0],
        "200": m200,
        "010": whole(t10),
        "110": t10[2] - t10[0],
        "020": whole(t20),
        "001": whole(t01),
        "101": t01[2] - t01[0],
        "011": whole(t11),
        "002": whole(t02),
    }


def line(o0, o1, o2, v):
    if o1 is None:
        d = v * o0
        e = o2 + v * d
    else:
        d = o1 + v * o0
        e = o2 + v * (o1 + d)
    return e - d, 0.5 * (o0 - e), e + d


def odd_line(o1, v):
    c = v * o1
    e = c + c
    return e - o1, -c, e + o1


def collided(m, omega):
    inv_m = 1.0 / m["000"]
    ux, uy, uz = m["100"] * inv_m, m["010"] * inv_m, m["001"] * inv_m
    n = {k: 0.125 * v for k, v in m.items()}
    rho, mx, my, mz = n["000"], n["100"], n["010"], n["001"]
    inverse = 8.0 * inv_m
    retain = 1.0 - omega
    c200 = n["200"] - mx * ux
    c020 = n["020"] - my * uy
    c002 = n["002"] - mz * uz
    third = 1.0 / 3.0
    d1 = retain * (c200 - c020)
    d2 = retain * (c200 - c002)
    total = rho + d1 + d2
    kxx = total * third
    kyy = (total - 3.0 * d1) * third
    kzz = (total - 3.0 * d2) * third
    kxy = retain * (n["110"] - mx * uy)
    kxz = retain * (n["101"] - mx * uz)
    kyz = retain * (n["011"] - my * uz)
    sxy, sxz, syz = kxy * kxy, kxz * kxz, kyz * kyz
    xy_xz, xy_yz, xz_yz = kxy * kxz, kxy * kyz, kxz * kyz
    k220 = (kxx * kyy + 2.0 * sxy) * inverse
    k202 = (kxx * kzz + 2.0 * sxz) * inverse
    yy_zz = kyy * kzz
    k022 = (yy_zz + 2.0 * syz) * inverse
    k211 = (kxx * kyz + 2.0 * xy_xz) * inverse
    k121 = (kyy * kxz + 2.0 * xy_yz) * inverse
    k112 = (kzz * kxy + 2.0 * xz_yz) * inverse
    k222 = (
        kxx * (yy_zz + 2.0 * syz) + 2.0 * (kyy * sxz + kzz * sxy) + 8.0 * (kxy * xz_yz)
    ) * (inverse * inverse)
    cols = {
        (0, 0): line(rho, None, kxx, ux),
        (1, 0): odd_line(kxy, ux),
        (2, 0): line(kyy, None, k220, ux),
        (0, 1): odd_line(kxz, ux),
        (1, 1): line(kyz, None, k211, ux),
        (2, 1): odd_line(k121, ux),
        (0, 2): line(kzz, None, k202, ux),
        (1, 2): odd_line(k112, ux),
        (2, 2): line(k022, None, k222, ux),
    }
    for a in range(3):
        by_y = [line(cols[0, c][a], cols[1, c][a], cols[2, c][a], uy) for c in range(3)]
        for b in range(3):
            ends = line(by_y[0][b], by_y[1][b], by_y[2][b], uz)
            for c in range(3):
                yield 9 * a + 3 * b + c, ends[c]


def kernel(
    n_gx,
    n_gy,
    count_ref,
    site_ref,
    patch_ref,
    pop_hbm,
    omega_hbm,
    walls_hbm,
    rad_hbm,
    bins_hbm,
    adv_ref,
    sig_ref,
    f_ref,
    rel,
    omega,
    walls,
    rad,
    bins,
    xsend,
    xrecv,
    ystage,
    ysend,
    yrecv,
    csend,
    crecv,
    lv_own,
    lv_gy,
    lv_sum,
    lv_in,
    one_hot,
    fields,
    rows,
    resp,
    resp_in,
    load_sem,
    halo_send,
    halo_recv,
    lvg_send,
    lvg_recv,
    lva_send,
    lva_recv,
    row_send,
    row_recv,
    resp_send,
    resp_recv,
):
    me_x, me_y = lax.axis_index("gx"), lax.axis_index("gy")

    def at_x(d):
        return lax.rem(me_x + (d + n_gx), n_gx)

    def at_y(d):
        return lax.rem(me_y + (d + n_gy), n_gy)

    layers = (3, 0, 1, 2)
    pop_loads = [
        pltpu.make_async_copy(pop_hbm.at[:, x], f_ref.at[:, x], load_sem.at[x]) for x in range(CX)
    ]
    omega_load = pltpu.make_async_copy(omega_hbm, omega, load_sem.at[4])
    walls_load = pltpu.make_async_copy(walls_hbm, walls, load_sem.at[5])
    bins_load = pltpu.make_async_copy(
        bins_hbm.at[:, pl.ds(pl.multiple_of(me_y * COLUMN, COLUMN), COLUMN)], bins, load_sem.at[6]
    )
    rad_load = pltpu.make_async_copy(rad_hbm.at[:, me_y], rad, load_sem.at[7])
    bins_load.start()
    omega_load.start()
    walls_load.start()
    for x in layers:
        pop_loads[x].start()
    rad_load.start()

    barrier = pltpu.get_barrier_semaphore()

    @pl.loop(1, n_gx)
    def _(d):
        pl.semaphore_signal(barrier, inc=1, device_id=(at_x(d), me_y), device_id_type=MESH)

    for e in range(1, n_gy):
        pl.semaphore_signal(barrier, inc=1, device_id=(me_x, at_y(e)), device_id_type=MESH)
    for sx, sy in CORNERS:
        pl.semaphore_signal(barrier, inc=1, device_id=(at_x(sx), at_y(sy)), device_id_type=MESH)

    def collide(s, first, layers):
        @pl.loop(0, 4 * layers)
        def _(j):
            x = first + j // 4
            y0 = pl.multiple_of(((j // 2) % 2) * 8, 8)
            z0 = pl.multiple_of((j % 2) * 128, 128)

            def g(a, b, c):
                return f_ref[9 * a + 3 * b + c, x, pl.ds(y0, 8), pl.ds(z0, 128)]

            m = moments(g)
            solid = walls[x, pl.ds(y0, 8), pl.ds(z0, 128)] == 1
            if s == 1:
                put_fields(m, x, y0, j % 2)
            for i, value in collided(m, omega[x, pl.ds(y0, 8), pl.ds(z0, 128)]):
                rel[s, i, x + 1, pl.ds(y0 + 8, 8), pl.ds(z0, 128)] = jnp.where(solid, WALL, value)

    def put_fields(m, x, y0, half):
        row = pl.multiple_of(half * 64 + x * CY + y0, 8)
        scale = 1.0 / 216.0
        fields[0, pl.ds(row, 8), :] = m["000"] * scale - 1.0
        fields[1, pl.ds(row, 8), :] = m["100"] * scale
        fields[2, pl.ds(row, 8), :] = m["010"] * scale
        fields[3, pl.ds(row, 8), :] = m["001"] * scale

    def x_copy(s, side):
        sx = 2 * side - 1
        return pltpu.make_async_remote_copy(
            src_ref=xsend.at[s, side],
            dst_ref=xrecv.at[s, side],
            send_sem=halo_send.at[s, side],
            recv_sem=halo_recv.at[s, side],
            device_id=(at_x(sx), me_y),
            device_id_type=MESH,
        )

    def y_copy(s, side):
        sy = 2 * side - 1
        return pltpu.make_async_remote_copy(
            src_ref=ysend.at[s, side],
            dst_ref=yrecv.at[s, side],
            send_sem=halo_send.at[s, 2 + side],
            recv_sem=halo_recv.at[s, 2 + side],
            device_id=(me_x, at_y(sy)),
            device_id_type=MESH,
        )

    def c_copy(s, corner):
        sx, sy = CORNERS[corner]
        return pltpu.make_async_remote_copy(
            src_ref=csend.at[s, corner, pl.ds(0, 3)],
            dst_ref=crecv.at[s, corner, pl.ds(0, 3)],
            send_sem=halo_send.at[s, 4 + corner],
            recv_sem=halo_recv.at[s, 4 + corner],
            device_id=(at_x(sx), at_y(sy)),
            device_id_type=MESH,
        )

    def crossing(sy):
        return [9 * a + 3 * (sy + 1) + c for a in range(3) for c in range(3)]

    def send_x(s, side):
        for j in range(9):
            value = rel[s, 18 * side + j, 1 + 3 * side, pl.ds(8, CY), :]
            xsend[s, side, j] = (value - 1.0).astype(BF16)
        x_copy(s, side).start()

    def send_y(s):
        for side in range(2):
            edge = 8 + 15 * side
            for j, i in enumerate(crossing(2 * side - 1)):
                for x in range(CX):
                    at = 4 * j + x
                    ystage[side, at : at + 1, :] = rel[s, i, x + 1, edge : edge + 1, :]
            ysend[s, side] = (ystage[side] - 1.0).astype(BF16)
            y_copy(s, side).start()

    def send_corners(s):
        for corner, (sx, sy) in enumerate(CORNERS):
            edge = 23 if sy > 0 else 8
            x = 4 if sx > 0 else 1
            for c in range(3):
                i = 9 * (sx + 1) + 3 * (sy + 1) + c
                csend[s, corner, c : c + 1, :] = rel[s, i, x, edge : edge + 1, :]
            c_copy(s, corner).start()

    def take_y(s):
        for side in range(2):
            y_copy(s, side).wait()
            ystage[side] = yrecv[s, side].astype(F32) + 1.0
            edge = 7 if side == 1 else 24
            for j, i in enumerate(crossing(2 * side - 1)):
                for x in range(CX):
                    at = 4 * j + x
                    rel[s, i, x + 1, edge : edge + 1, :] = ystage[side, at : at + 1, :]

    def take_x(s):
        for corner, (sx, sy) in enumerate(CORNERS):
            c_copy(s, corner).wait()
            edge = 7 if sy > 0 else 24
            x = 0 if sx > 0 else 5
            for c in range(3):
                i = 9 * (sx + 1) + 3 * (sy + 1) + c
                rel[s, i, x, edge : edge + 1, :] = crecv[s, corner, c : c + 1, :]
        for side in range(2):
            x_copy(s, side).wait()
            for j in range(9):
                rel[s, 18 * side + j, 5 - 5 * side, pl.ds(8, CY), :] = (
                    xrecv[s, side, j].astype(F32) + 1.0
                )

    def stream(s, first, step):
        to_ref = adv_ref if s == 1 else f_ref

        @pl.loop(0, 2)
        def _(j):
            x = first + j * step
            solid = walls[x] == 1
            for i in range(27):
                cx, cy, cz = i // 9 - 1, (i // 3) % 3 - 1, i % 3 - 1
                source = rel[s, i, x + 1 - cx, pl.ds(8 - cy, CY), :]
                if cz:
                    source = pltpu.roll(source, cz % NZ, 1)
                bounced = jnp.where(
                    source > WALL_TEST, rel[s, 26 - i, x + 1, pl.ds(8, CY), :], source
                )
                to_ref[i, x] = jnp.where(solid, f_ref[i, x], bounced)

    def late_fields(first, step):
        @pl.loop(0, 8)
        def _(j):
            x = first + (j // 4) * step
            y0 = pl.multiple_of(((j // 2) % 2) * 8, 8)
            z0 = pl.multiple_of((j % 2) * 128, 128)

            def g(a, b, c):
                return adv_ref[9 * a + 3 * b + c, x, pl.ds(y0, 8), pl.ds(z0, 128)]

            put_fields(moments(g), x, y0, j % 2)

    def send_rows(s):
        for part in range(4):
            taken = jnp.dot(selector, fields[part].astype(BF16), preferred_element_type=F32)
            rows[s, me_y, :, part * ZS : (part + 1) * ZS] = taken.astype(BF16)
        for e in range(1, n_gy):
            row_copy(s, e).start()

    def row_copy(s, e):
        return pltpu.make_async_remote_copy(
            src_ref=rows.at[s, me_y],
            dst_ref=rows.at[s, me_y],
            send_sem=row_send.at[s, e],
            recv_sem=row_recv.at[s, e],
            device_id=(me_x, at_y(e)),
            device_id_type=MESH,
        )

    def take_rows(s):
        for e in range(1, n_gy):
            pltpu.make_async_remote_copy(
                src_ref=rows.at[s, me_y],
                dst_ref=rows.at[s, at_y(-e)],
                send_sem=row_send.at[s, e],
                recv_sem=row_recv.at[s, e],
                device_id=(me_x, at_y(e)),
                device_id_type=MESH,
            ).wait()

    def lvg_copy(e):
        return pltpu.make_async_remote_copy(
            src_ref=lv_own,
            dst_ref=lv_gy.at[e],
            send_sem=lvg_send.at[e],
            recv_sem=lvg_recv.at[e],
            device_id=(me_x, at_y(e)),
            device_id_type=MESH,
        )

    def lva_copy(d):
        return pltpu.make_async_remote_copy(
            src_ref=lv_sum.at[at_x(d)],
            dst_ref=lv_in.at[d],
            send_sem=lva_send.at[d],
            recv_sem=lva_recv.at[d],
            device_id=(at_x(d), me_y),
            device_id_type=MESH,
        )

    def resp_copy(d):
        return pltpu.make_async_remote_copy(
            src_ref=resp.at[at_x(d)],
            dst_ref=resp_in.at[d],
            send_sem=resp_send.at[d],
            recv_sem=resp_recv.at[d],
            device_id=(at_x(d), me_y),
            device_id_type=MESH,
        )

    omega_load.wait()
    walls_load.wait()
    pop_loads[3].wait()
    collide(0, 3, 1)
    pl.semaphore_wait(barrier, n_gx - 1 + n_gy - 1 + 4)
    send_x(0, 1)
    pop_loads[0].wait()
    collide(0, 0, 1)
    send_x(0, 0)
    pop_loads[1].wait()
    pop_loads[2].wait()
    collide(0, 1, 2)
    send_y(0)
    send_corners(0)

    lane = lax.broadcasted_iota(jnp.int32, (COLUMN, 128), 1)
    sub = lax.broadcasted_iota(jnp.int32, (COLUMN, 128), 0)
    slot_patch = jnp.full((COLUMN, 128), -1, jnp.int32)
    for k in range(SAMP):
        local = patch_ref[0, k] - me_y * COLUMN
        slot_patch = jnp.where(lane % 64 == me_y * SAMP + k, local, slot_patch)
    pick = (slot_patch == sub).astype(BF16)
    bins_load.wait()
    level = lax.dot_general(
        bins[...].astype(F32).astype(BF16), pick, (((1,), (0,)), ((), ())), preferred_element_type=F32
    )
    lane_b = lax.broadcasted_iota(jnp.int32, (n_gx, 128), 1)
    later = (lane_b >= 64) & ((lane_b % 64) // SAMP == me_y)
    level = level + jnp.where(later, 1.0, 0.0)
    for b in range(n_gx):
        lv_own[b] = level[b : b + 1, :]
    for e in range(1, n_gy):
        lvg_copy(e).start()

    sub_k = lax.broadcasted_iota(jnp.int32, (SAMP, 128), 0)
    lane_k = lax.broadcasted_iota(jnp.int32, (SAMP, 128), 1)
    target = jnp.full((SAMP, 128), -1, jnp.int32)
    for k in range(SAMP):
        site = site_ref[0, k]
        target = jnp.where(sub_k == k, (site % 2) * 64 + site // 2, target)
    live = (target == lane_k) & (sub_k < count_ref[0, 0])
    selector = live.astype(BF16)

    summed = lv_own[...]
    for e in range(1, n_gy):
        lvg_copy(e).wait()
        summed = summed + lv_gy[e]
    lv_sum[...] = summed

    @pl.loop(1, n_gx)
    def _(d):
        lva_copy(d).start()

    lv_in[0] = lv_sum[me_x]
    take_y(0)
    stream(0, 1, 1)
    collide(1, 1, 2)
    take_x(0)
    stream(0, 0, 3)
    collide(1, 3, 1)
    send_x(1, 1)
    collide(1, 0, 1)
    send_x(1, 0)
    send_y(1)
    send_corners(1)
    send_rows(0)

    @pl.loop(0, n_gx)
    def _(d):
        @pl.when(d > 0)
        def _():
            lva_copy(d).wait()

        wanted = lax.broadcasted_iota(jnp.int32, (LEVELS, 128), 0).astype(F32)
        one_hot[d] = (jnp.broadcast_to(lv_in[d], (LEVELS, 128)) == wanted).astype(BF16)

    take_rows(0)
    rad_load.wait()
    take_y(1)
    stream(1, 1, 1)
    late_fields(1, 1)
    take_x(1)
    stream(1, 0, 3)
    late_fields(0, 3)
    send_rows(1)
    take_rows(1)
    all_rows = rows[...].reshape(2 * n_gy * SAMP, 4 * ZS)

    seen = lax.dot_general(
        rad[...].reshape(n_gx * OWN, 4 * ZS),
        all_rows,
        (((1,), (1,)), ((), ())),
        preferred_element_type=F32,
    )
    resp[...] = seen.astype(BF16).reshape(n_gx, OWN, 128)

    @pl.loop(1, n_gx)
    def _(d):
        resp_copy(d).start()

    resp_in[0] = resp[me_x]
    per = max(n_gx // 8, 1)
    total = jnp.zeros((OWN, LEVELS), F32)
    for start in range(0, n_gx // 2, per):
        group = list(range(start, start + per)) + list(range(n_gx - start - per, n_gx - start))
        for d in group:
            if d > 0:
                resp_copy(d).wait()
        total = total + lax.dot_general(
            jnp.concatenate([resp_in[d] for d in group], axis=1),
            jnp.concatenate([one_hot[d] for d in group], axis=1),
            (((1,), (1,)), ((), ())),
            preferred_element_type=F32,
        )
    sig_ref[...] = total


def finish(adv_in, sig_in, adv_out, sig_out, sem):
    copies = [
        pltpu.make_async_copy(adv_in.at[pl.ds(9 * a, 9)], adv_out.at[pl.ds(9 * a, 9)], sem.at[a])
        for a in range(3)
    ]
    copies.append(pltpu.make_async_copy(sig_in, sig_out, sem.at[3]))
    for copy in copies:
        copy.start()
    for copy in copies:
        copy.wait()


def per_device(populations, omega, walls, radiation, bins, counts, sample_site, sample_patch):
    n_gx, n_gy = lax.axis_size("gx"), lax.axis_size("gy")
    hbm = pl.BlockSpec(memory_space=pl.ANY)
    smem = pl.BlockSpec(memory_space=pltpu.SMEM)
    vmem = pl.BlockSpec(memory_space=pltpu.VMEM)
    dma = pltpu.SemaphoreType.DMA
    scratch = [
        pltpu.VMEM((27, CX, CY, NZ), F32),
        pltpu.VMEM((2, 27, CX + 2, CY + 16, NZ), F32),
        pltpu.VMEM((CX, CY, NZ), F32),
        pltpu.VMEM((CX, CY, NZ), jnp.int32),
        pltpu.VMEM((n_gx, OWN, 4 * ZS), BF16),
        pltpu.VMEM((n_gx, COLUMN), jnp.int32),
        pltpu.VMEM((2, 2, 9, CY, NZ), BF16),
        pltpu.VMEM((2, 2, 9, CY, NZ), BF16),
        pltpu.VMEM((2, 9 * CX, NZ), F32),
        pltpu.VMEM((2, 2, 9 * CX, NZ), BF16),
        pltpu.VMEM((2, 2, 9 * CX, NZ), BF16),
        pltpu.VMEM((2, 4, 8, NZ), F32),
        pltpu.VMEM((2, 4, 8, NZ), F32),
        pltpu.VMEM((n_gx, 1, 128), F32),
        pltpu.VMEM((n_gy, n_gx, 1, 128), F32),
        pltpu.VMEM((n_gx, 1, 128), F32),
        pltpu.VMEM((n_gx, 1, 128), F32),
        pltpu.VMEM((n_gx, LEVELS, 128), BF16),
        pltpu.VMEM((4, 128, ZS), F32),
        pltpu.VMEM((2, n_gy, SAMP, 4 * ZS), BF16),
        pltpu.VMEM((n_gx, OWN, 128), BF16),
        pltpu.VMEM((n_gx, OWN, 128), BF16),
        dma((8,)),
        dma((2, 8)),
        dma((2, 8)),
        dma((n_gy,)),
        dma((n_gy,)),
        dma((n_gx,)),
        dma((n_gx,)),
        dma((2, n_gy)),
        dma((2, n_gy)),
        dma((n_gx,)),
        dma((n_gx,)),
    ]
    operands = (
        sample_site.reshape(1, SAMP),
        sample_patch.reshape(1, SAMP),
        populations,
        omega,
        walls,
        radiation.reshape(n_gx, n_gy, OWN, 4 * ZS),
        bins.T,
    )
    advanced, signal = pl.pallas_call(
        functools.partial(kernel, n_gx, n_gy),
        out_shape=(
            jax.ShapeDtypeStruct((27, CX, CY, NZ), F32),
            jax.ShapeDtypeStruct((OWN, LEVELS), F32),
        ),
        in_specs=[smem] * 3 + [hbm] * 5,
        out_specs=(vmem, vmem),
        scratch_shapes=scratch,
        compiler_params=pltpu.CompilerParams(
            collective_id=0, has_side_effects=True, vmem_limit_bytes=44 * 2**20
        ),
        name="lattice_far_field",
    )(counts, *[pltpu.with_memory_space_constraint(x, pltpu.HBM) for x in operands])
    return pl.pallas_call(
        finish,
        out_shape=(
            jax.ShapeDtypeStruct((27, CX, CY, NZ), F32),
            jax.ShapeDtypeStruct((OWN, LEVELS), F32),
        ),
        in_specs=[hbm] * 2,
        out_specs=(hbm, hbm),
        scratch_shapes=[dma((4,))],
        compiler_params=pltpu.CompilerParams(vmem_limit_bytes=2**20),
        name="write_out",
    )(advanced, signal)


def solution(mesh):
    return jax.shard_map(
        per_device,
        mesh=mesh,
        in_specs=(
            P(None, "gx", "gy", None),
            P("gx", "gy", None),
            P("gx", "gy", None),
            P(),
            P(),
            P("gx", "gy"),
            P("gx", "gy", None),
            P("gx", "gy", None),
        ),
        out_specs=(P(None, "gx", "gy", None), P(("gx", "gy"), None)),
        check_vma=False,
    )
```

```python
import functools

import jax
import jax.numpy as jnp
from jax import lax
from jax.experimental import pallas as pl
from jax.experimental.pallas import tpu as pltpu
from jax.sharding import PartitionSpec as P

CX = 4
CY = 16
NZ = 256
ZS = 128
SAMP = 16
LEVELS = 128
COLUMN = 128
OWN = 32
WALL = 2.0**100
WALL_TEST = 2.0**60
MESH = pl.DeviceIdType.MESH
F32 = jnp.float32
BF16 = jnp.bfloat16
CORNERS = ((-1, -1), (-1, 1), (1, -1), (1, 1))


def moments(g):
    def pair(lo, hi):
        return lo + hi, hi - lo

    s0 = [[None] * 3 for _ in range(3)]
    s1 = [[None] * 3 for _ in range(3)]
    s2 = [[None] * 3 for _ in range(3)]
    for a in range(3):
        for b in range(3):
            lo, mid, hi = g(a, b, 0), g(a, b, 1), g(a, b, 2)
            s2[a][b], s1[a][b] = pair(lo, hi)
            s0[a][b] = 4.0 * mid + s2[a][b]
    t00, t10, t20, t01, t11, t02 = [], [], [], [], [], []
    for a in range(3):
        ends, gap = pair(s0[a][0], s0[a][2])
        t00.append(4.0 * s0[a][1] + ends)
        t10.append(gap)
        t20.append(ends)
        ends, gap = pair(s1[a][0], s1[a][2])
        t01.append(4.0 * s1[a][1] + ends)
        t11.append(gap)
        t02.append(4.0 * s2[a][1] + (s2[a][0] + s2[a][2]))

    def whole(t):
        return 4.0 * t[1] + (t[0] + t[2])

    m200 = t00[0] + t00[2]
    return {
        "000": 4.0 * t00[1] + m200,
        "100": t00[2] - t00[0],
        "200": m200,
        "010": whole(t10),
        "110": t10[2] - t10[0],
        "020": whole(t20),
        "001": whole(t01),
        "101": t01[2] - t01[0],
        "011": whole(t11),
        "002": whole(t02),
    }


def line(o0, o1, o2, v):
    if o1 is None:
        d = v * o0
        e = o2 + v * d
    else:
        d = o1 + v * o0
        e = o2 + v * (o1 + d)
    return e - d, 0.5 * (o0 - e), e + d


def odd_line(o1, v):
    c = v * o1
    e = c + c
    return e - o1, -c, e + o1


def collided(m, omega):
    inv_m = 1.0 / m["000"]
    ux, uy, uz = m["100"] * inv_m, m["010"] * inv_m, m["001"] * inv_m
    n = {k: 0.125 * v for k, v in m.items()}
    rho, mx, my, mz = n["000"], n["100"], n["010"], n["001"]
    inverse = 8.0 * inv_m
    retain = 1.0 - omega
    c200 = n["200"] - mx * ux
    c020 = n["020"] - my * uy
    c002 = n["002"] - mz * uz
    third = 1.0 / 3.0
    d1 = retain * (c200 - c020)
    d2 = retain * (c200 - c002)
    total = rho + d1 + d2
    kxx = total * third
    kyy = (total - 3.0 * d1) * third
    kzz = (total - 3.0 * d2) * third
    kxy = retain * (n["110"] - mx * uy)
    kxz = retain * (n["101"] - mx * uz)
    kyz = retain * (n["011"] - my * uz)
    sxy, sxz, syz = kxy * kxy, kxz * kxz, kyz * kyz
    xy_xz, xy_yz, xz_yz = kxy * kxz, kxy * kyz, kxz * kyz
    k220 = (kxx * kyy + 2.0 * sxy) * inverse
    k202 = (kxx * kzz + 2.0 * sxz) * inverse
    yy_zz = kyy * kzz
    k022 = (yy_zz + 2.0 * syz) * inverse
    k211 = (kxx * kyz + 2.0 * xy_xz) * inverse
    k121 = (kyy * kxz + 2.0 * xy_yz) * inverse
    k112 = (kzz * kxy + 2.0 * xz_yz) * inverse
    k222 = (
        kxx * (yy_zz + 2.0 * syz) + 2.0 * (kyy * sxz + kzz * sxy) + 8.0 * (kxy * xz_yz)
    ) * (inverse * inverse)
    cols = {
        (0, 0): line(rho, None, kxx, ux),
        (1, 0): odd_line(kxy, ux),
        (2, 0): line(kyy, None, k220, ux),
        (0, 1): odd_line(kxz, ux),
        (1, 1): line(kyz, None, k211, ux),
        (2, 1): odd_line(k121, ux),
        (0, 2): line(kzz, None, k202, ux),
        (1, 2): odd_line(k112, ux),
        (2, 2): line(k022, None, k222, ux),
    }
    for a in range(3):
        by_y = [line(cols[0, c][a], cols[1, c][a], cols[2, c][a], uy) for c in range(3)]
        for b in range(3):
            ends = line(by_y[0][b], by_y[1][b], by_y[2][b], uz)
            for c in range(3):
                yield 9 * a + 3 * b + c, ends[c]


def kernel(
    n_gx,
    n_gy,
    count_ref,
    site_ref,
    patch_ref,
    pop_hbm,
    omega_hbm,
    walls_hbm,
    rad_hbm,
    bins_hbm,
    adv_ref,
    sig_ref,
    f_ref,
    rel,
    omega,
    walls,
    rad,
    bins,
    xsend,
    xrecv,
    ystage,
    ysend,
    yrecv,
    csend,
    crecv,
    lv_own,
    lv_gy,
    lv_sum,
    lv_in,
    one_hot,
    fields,
    rows,
    resp,
    resp_in,
    load_sem,
    halo_send,
    halo_recv,
    lvg_send,
    lvg_recv,
    lva_send,
    lva_recv,
    row_send,
    row_recv,
    resp_send,
    resp_recv,
):
    me_x, me_y = lax.axis_index("gx"), lax.axis_index("gy")

    def at_x(d):
        return lax.rem(me_x + (d + n_gx), n_gx)

    def at_y(d):
        return lax.rem(me_y + (d + n_gy), n_gy)

    layers = (3, 0, 1, 2)
    pop_loads = [
        pltpu.make_async_copy(pop_hbm.at[:, x], f_ref.at[:, x], load_sem.at[x]) for x in range(CX)
    ]
    omega_load = pltpu.make_async_copy(omega_hbm, omega, load_sem.at[4])
    walls_load = pltpu.make_async_copy(walls_hbm, walls, load_sem.at[5])
    bins_load = pltpu.make_async_copy(
        bins_hbm.at[:, pl.ds(pl.multiple_of(me_y * COLUMN, COLUMN), COLUMN)], bins, load_sem.at[6]
    )
    rad_load = pltpu.make_async_copy(rad_hbm.at[:, me_y], rad, load_sem.at[7])
    bins_load.start()
    omega_load.start()
    walls_load.start()
    for x in layers:
        pop_loads[x].start()
    rad_load.start()

    barrier = pltpu.get_barrier_semaphore()

    @pl.loop(1, n_gx)
    def _(d):
        pl.semaphore_signal(barrier, inc=1, device_id=(at_x(d), me_y), device_id_type=MESH)

    for e in range(1, n_gy):
        pl.semaphore_signal(barrier, inc=1, device_id=(me_x, at_y(e)), device_id_type=MESH)
    for sx, sy in CORNERS:
        pl.semaphore_signal(barrier, inc=1, device_id=(at_x(sx), at_y(sy)), device_id_type=MESH)

    def collide(s, first, layers):
        @pl.loop(0, 4 * layers)
        def _(j):
            x = first + j // 4
            y0 = pl.multiple_of(((j // 2) % 2) * 8, 8)
            z0 = pl.multiple_of((j % 2) * 128, 128)

            def g(a, b, c):
                return f_ref[9 * a + 3 * b + c, x, pl.ds(y0, 8), pl.ds(z0, 128)]

            m = moments(g)
            solid = walls[x, pl.ds(y0, 8), pl.ds(z0, 128)] == 1
            if s == 1:
                put_fields(m, x, y0, j % 2)
            for i, value in collided(m, omega[x, pl.ds(y0, 8), pl.ds(z0, 128)]):
                rel[s, i, x + 1, pl.ds(y0 + 8, 8), pl.ds(z0, 128)] = jnp.where(solid, WALL, value)

    def put_fields(m, x, y0, half):
        row = pl.multiple_of(half * 64 + x * CY + y0, 8)
        scale = 1.0 / 216.0
        fields[0, pl.ds(row, 8), :] = m["000"] * scale - 1.0
        fields[1, pl.ds(row, 8), :] = m["100"] * scale
        fields[2, pl.ds(row, 8), :] = m["010"] * scale
        fields[3, pl.ds(row, 8), :] = m["001"] * scale

    def x_copy(s, side):
        sx = 2 * side - 1
        return pltpu.make_async_remote_copy(
            src_ref=xsend.at[s, side],
            dst_ref=xrecv.at[s, side],
            send_sem=halo_send.at[s, side],
            recv_sem=halo_recv.at[s, side],
            device_id=(at_x(sx), me_y),
            device_id_type=MESH,
        )

    def y_copy(s, side):
        sy = 2 * side - 1
        return pltpu.make_async_remote_copy(
            src_ref=ysend.at[s, side],
            dst_ref=yrecv.at[s, side],
            send_sem=halo_send.at[s, 2 + side],
            recv_sem=halo_recv.at[s, 2 + side],
            device_id=(me_x, at_y(sy)),
            device_id_type=MESH,
        )

    def c_copy(s, corner):
        sx, sy = CORNERS[corner]
        return pltpu.make_async_remote_copy(
            src_ref=csend.at[s, corner, pl.ds(0, 3)],
            dst_ref=crecv.at[s, corner, pl.ds(0, 3)],
            send_sem=halo_send.at[s, 4 + corner],
            recv_sem=halo_recv.at[s, 4 + corner],
            device_id=(at_x(sx), at_y(sy)),
            device_id_type=MESH,
        )

    def crossing(sy):
        return [9 * a + 3 * (sy + 1) + c for a in range(3) for c in range(3)]

    def send_x(s, side):
        for j in range(9):
            value = rel[s, 18 * side + j, 1 + 3 * side, pl.ds(8, CY), :]
            xsend[s, side, j] = (value - 1.0).astype(BF16)
        x_copy(s, side).start()

    def send_y(s):
        for side in range(2):
            edge = 8 + 15 * side
            for j, i in enumerate(crossing(2 * side - 1)):
                for x in range(CX):
                    at = 4 * j + x
                    ystage[side, at : at + 1, :] = rel[s, i, x + 1, edge : edge + 1, :]
            ysend[s, side] = (ystage[side] - 1.0).astype(BF16)
            y_copy(s, side).start()

    def send_corners(s):
        for corner, (sx, sy) in enumerate(CORNERS):
            edge = 23 if sy > 0 else 8
            x = 4 if sx > 0 else 1
            for c in range(3):
                i = 9 * (sx + 1) + 3 * (sy + 1) + c
                csend[s, corner, c : c + 1, :] = rel[s, i, x, edge : edge + 1, :]
            c_copy(s, corner).start()

    def take_y(s):
        for side in range(2):
            y_copy(s, side).wait()
            ystage[side] = yrecv[s, side].astype(F32) + 1.0
            edge = 7 if side == 1 else 24
            for j, i in enumerate(crossing(2 * side - 1)):
                for x in range(CX):
                    at = 4 * j + x
                    rel[s, i, x + 1, edge : edge + 1, :] = ystage[side, at : at + 1, :]

    def take_x(s):
        for corner, (sx, sy) in enumerate(CORNERS):
            c_copy(s, corner).wait()
            edge = 7 if sy > 0 else 24
            x = 0 if sx > 0 else 5
            for c in range(3):
                i = 9 * (sx + 1) + 3 * (sy + 1) + c
                rel[s, i, x, edge : edge + 1, :] = crecv[s, corner, c : c + 1, :]
        for side in range(2):
            x_copy(s, side).wait()
            for j in range(9):
                rel[s, 18 * side + j, 5 - 5 * side, pl.ds(8, CY), :] = (
                    xrecv[s, side, j].astype(F32) + 1.0
                )

    def stream(s, first, step):
        to_ref = adv_ref if s == 1 else f_ref

        @pl.loop(0, 2)
        def _(j):
            x = first + j * step
            solid = walls[x] == 1
            for i in range(27):
                cx, cy, cz = i // 9 - 1, (i // 3) % 3 - 1, i % 3 - 1
                source = rel[s, i, x + 1 - cx, pl.ds(8 - cy, CY), :]
                if cz:
                    source = pltpu.roll(source, cz % NZ, 1)
                bounced = jnp.where(
                    source > WALL_TEST, rel[s, 26 - i, x + 1, pl.ds(8, CY), :], source
                )
                to_ref[i, x] = jnp.where(solid, f_ref[i, x], bounced)

    def late_fields(first, step):
        @pl.loop(0, 8)
        def _(j):
            x = first + (j // 4) * step
            y0 = pl.multiple_of(((j // 2) % 2) * 8, 8)
            z0 = pl.multiple_of((j % 2) * 128, 128)

            def g(a, b, c):
                return adv_ref[9 * a + 3 * b + c, x, pl.ds(y0, 8), pl.ds(z0, 128)]

            put_fields(moments(g), x, y0, j % 2)

    def send_rows(s):
        for part in range(4):
            taken = jnp.dot(selector, fields[part].astype(BF16), preferred_element_type=F32)
            rows[s, me_y, :, part * ZS : (part + 1) * ZS] = taken.astype(BF16)
        for e in range(1, n_gy):
            row_copy(s, e).start()

    def row_copy(s, e):
        return pltpu.make_async_remote_copy(
            src_ref=rows.at[s, me_y],
            dst_ref=rows.at[s, me_y],
            send_sem=row_send.at[s, e],
            recv_sem=row_recv.at[s, e],
            device_id=(me_x, at_y(e)),
            device_id_type=MESH,
        )

    def take_rows(s):
        for e in range(1, n_gy):
            pltpu.make_async_remote_copy(
                src_ref=rows.at[s, me_y],
                dst_ref=rows.at[s, at_y(-e)],
                send_sem=row_send.at[s, e],
                recv_sem=row_recv.at[s, e],
                device_id=(me_x, at_y(e)),
                device_id_type=MESH,
            ).wait()

    def lvg_copy(e):
        return pltpu.make_async_remote_copy(
            src_ref=lv_own,
            dst_ref=lv_gy.at[e],
            send_sem=lvg_send.at[e],
            recv_sem=lvg_recv.at[e],
            device_id=(me_x, at_y(e)),
            device_id_type=MESH,
        )

    def lva_copy(d):
        return pltpu.make_async_remote_copy(
            src_ref=lv_sum.at[at_x(d)],
            dst_ref=lv_in.at[d],
            send_sem=lva_send.at[d],
            recv_sem=lva_recv.at[d],
            device_id=(at_x(d), me_y),
            device_id_type=MESH,
        )

    def resp_copy(d):
        return pltpu.make_async_remote_copy(
            src_ref=resp.at[at_x(d)],
            dst_ref=resp_in.at[d],
            send_sem=resp_send.at[d],
            recv_sem=resp_recv.at[d],
            device_id=(at_x(d), me_y),
            device_id_type=MESH,
        )

    omega_load.wait()
    walls_load.wait()
    pop_loads[3].wait()
    collide(0, 3, 1)
    pl.semaphore_wait(barrier, n_gx - 1 + n_gy - 1 + 4)
    send_x(0, 1)
    pop_loads[0].wait()
    collide(0, 0, 1)
    send_x(0, 0)
    pop_loads[1].wait()
    pop_loads[2].wait()
    collide(0, 1, 2)
    send_y(0)
    send_corners(0)

    lane = lax.broadcasted_iota(jnp.int32, (COLUMN, 128), 1)
    sub = lax.broadcasted_iota(jnp.int32, (COLUMN, 128), 0)
    slot_patch = jnp.full((COLUMN, 128), -1, jnp.int32)
    for k in range(SAMP):
        local = patch_ref[0, k] - me_y * COLUMN
        slot_patch = jnp.where(lane % 64 == me_y * SAMP + k, local, slot_patch)
    pick = (slot_patch == sub).astype(BF16)
    bins_load.wait()
    level = lax.dot_general(
        bins[...].astype(F32).astype(BF16), pick, (((1,), (0,)), ((), ())), preferred_element_type=F32
    )
    lane_b = lax.broadcasted_iota(jnp.int32, (n_gx, 128), 1)
    later = (lane_b >= 64) & ((lane_b % 64) // SAMP == me_y)
    level = level + jnp.where(later, 1.0, 0.0)
    for b in range(n_gx):
        lv_own[b] = level[b : b + 1, :]
    for e in range(1, n_gy):
        lvg_copy(e).start()

    sub_k = lax.broadcasted_iota(jnp.int32, (SAMP, 128), 0)
    lane_k = lax.broadcasted_iota(jnp.int32, (SAMP, 128), 1)
    target = jnp.full((SAMP, 128), -1, jnp.int32)
    for k in range(SAMP):
        site = site_ref[0, k]
        target = jnp.where(sub_k == k, (site % 2) * 64 + site // 2, target)
    live = (target == lane_k) & (sub_k < count_ref[0, 0])
    selector = live.astype(BF16)

    take_y(0)
    stream(0, 1, 1)
    collide(1, 1, 2)
    take_x(0)
    stream(0, 0, 3)
    collide(1, 3, 1)
    send_x(1, 1)
    collide(1, 0, 1)
    send_x(1, 0)
    send_y(1)
    send_corners(1)
    send_rows(0)

    summed = lv_own[...]
    for e in range(1, n_gy):
        lvg_copy(e).wait()
        summed = summed + lv_gy[e]
    lv_sum[...] = summed

    @pl.loop(1, n_gx)
    def _(d):
        lva_copy(d).start()

    lv_in[0] = lv_sum[me_x]
    take_rows(0)
    rad_load.wait()
    take_y(1)
    stream(1, 1, 1)
    late_fields(1, 1)
    take_x(1)
    stream(1, 0, 3)
    late_fields(0, 3)
    send_rows(1)
    take_rows(1)
    all_rows = rows[...].reshape(2 * n_gy * SAMP, 4 * ZS)

    seen = lax.dot_general(
        rad[...].reshape(n_gx * OWN, 4 * ZS),
        all_rows,
        (((1,), (1,)), ((), ())),
        preferred_element_type=F32,
    )
    resp[...] = seen.astype(BF16).reshape(n_gx, OWN, 128)

    @pl.loop(1, n_gx)
    def _(d):
        resp_copy(d).start()

    resp_in[0] = resp[me_x]

    @pl.loop(0, n_gx)
    def _(d):
        @pl.when(d > 0)
        def _():
            lva_copy(d).wait()

        wanted = lax.broadcasted_iota(jnp.int32, (LEVELS, 128), 0).astype(F32)
        one_hot[d] = (jnp.broadcast_to(lv_in[d], (LEVELS, 128)) == wanted).astype(BF16)

    per = max(n_gx // 8, 1)
    total = jnp.zeros((OWN, LEVELS), F32)
    for start in range(0, n_gx // 2, per):
        group = list(range(start, start + per)) + list(range(n_gx - start - per, n_gx - start))
        for d in group:
            if d > 0:
                resp_copy(d).wait()
        total = total + lax.dot_general(
            jnp.concatenate([resp_in[d] for d in group], axis=1),
            jnp.concatenate([one_hot[d] for d in group], axis=1),
            (((1,), (1,)), ((), ())),
            preferred_element_type=F32,
        )
    sig_ref[...] = total


def finish(adv_in, sig_in, adv_out, sig_out, sem):
    copies = [
        pltpu.make_async_copy(adv_in.at[pl.ds(9 * a, 9)], adv_out.at[pl.ds(9 * a, 9)], sem.at[a])
        for a in range(3)
    ]
    copies.append(pltpu.make_async_copy(sig_in, sig_out, sem.at[3]))
    for copy in copies:
        copy.start()
    for copy in copies:
        copy.wait()


def per_device(populations, omega, walls, radiation, bins, counts, sample_site, sample_patch):
    n_gx, n_gy = lax.axis_size("gx"), lax.axis_size("gy")
    hbm = pl.BlockSpec(memory_space=pl.ANY)
    smem = pl.BlockSpec(memory_space=pltpu.SMEM)
    vmem = pl.BlockSpec(memory_space=pltpu.VMEM)
    dma = pltpu.SemaphoreType.DMA
    scratch = [
        pltpu.VMEM((27, CX, CY, NZ), F32),
        pltpu.VMEM((2, 27, CX + 2, CY + 16, NZ), F32),
        pltpu.VMEM((CX, CY, NZ), F32),
        pltpu.VMEM((CX, CY, NZ), jnp.int32),
        pltpu.VMEM((n_gx, OWN, 4 * ZS), BF16),
        pltpu.VMEM((n_gx, COLUMN), jnp.int32),
        pltpu.VMEM((2, 2, 9, CY, NZ), BF16),
        pltpu.VMEM((2, 2, 9, CY, NZ), BF16),
        pltpu.VMEM((2, 9 * CX, NZ), F32),
        pltpu.VMEM((2, 2, 9 * CX, NZ), BF16),
        pltpu.VMEM((2, 2, 9 * CX, NZ), BF16),
        pltpu.VMEM((2, 4, 8, NZ), F32),
        pltpu.VMEM((2, 4, 8, NZ), F32),
        pltpu.VMEM((n_gx, 1, 128), F32),
        pltpu.VMEM((n_gy, n_gx, 1, 128), F32),
        pltpu.VMEM((n_gx, 1, 128), F32),
        pltpu.VMEM((n_gx, 1, 128), F32),
        pltpu.VMEM((n_gx, LEVELS, 128), BF16),
        pltpu.VMEM((4, 128, ZS), F32),
        pltpu.VMEM((2, n_gy, SAMP, 4 * ZS), BF16),
        pltpu.VMEM((n_gx, OWN, 128), BF16),
        pltpu.VMEM((n_gx, OWN, 128), BF16),
        dma((8,)),
        dma((2, 8)),
        dma((2, 8)),
        dma((n_gy,)),
        dma((n_gy,)),
        dma((n_gx,)),
        dma((n_gx,)),
        dma((2, n_gy)),
        dma((2, n_gy)),
        dma((n_gx,)),
        dma((n_gx,)),
    ]
    operands = (
        sample_site.reshape(1, SAMP),
        sample_patch.reshape(1, SAMP),
        populations,
        omega,
        walls,
        radiation.reshape(n_gx, n_gy, OWN, 4 * ZS),
        bins.T,
    )
    advanced, signal = pl.pallas_call(
        functools.partial(kernel, n_gx, n_gy),
        out_shape=(
            jax.ShapeDtypeStruct((27, CX, CY, NZ), F32),
            jax.ShapeDtypeStruct((OWN, LEVELS), F32),
        ),
        in_specs=[smem] * 3 + [hbm] * 5,
        out_specs=(vmem, vmem),
        scratch_shapes=scratch,
        compiler_params=pltpu.CompilerParams(
            collective_id=0, has_side_effects=True, vmem_limit_bytes=44 * 2**20
        ),
        name="lattice_far_field",
    )(counts, *[pltpu.with_memory_space_constraint(x, pltpu.HBM) for x in operands])
    return pl.pallas_call(
        finish,
        out_shape=(
            jax.ShapeDtypeStruct((27, CX, CY, NZ), F32),
            jax.ShapeDtypeStruct((OWN, LEVELS), F32),
        ),
        in_specs=[hbm] * 2,
        out_specs=(hbm, hbm),
        scratch_shapes=[dma((4,))],
        compiler_params=pltpu.CompilerParams(vmem_limit_bytes=2**20),
        name="write_out",
    )(advanced, signal)


def solution(mesh):
    return jax.shard_map(
        per_device,
        mesh=mesh,
        in_specs=(
            P(None, "gx", "gy", None),
            P("gx", "gy", None),
            P("gx", "gy", None),
            P(),
            P(),
            P("gx", "gy"),
            P("gx", "gy", None),
            P("gx", "gy", None),
        ),
        out_specs=(P(None, "gx", "gy", None), P(("gx", "gy"), None)),
        check_vma=False,
    )
```

```python
import functools

import jax
import jax.numpy as jnp
from jax import lax
from jax.experimental import pallas as pl
from jax.experimental.pallas import tpu as pltpu
from jax.sharding import PartitionSpec as P

CX = 4
CY = 16
NZ = 256
ZS = 128
SAMP = 16
LEVELS = 128
COLUMN = 128
OWN = 32
WALL = 2.0**100
WALL_TEST = 2.0**60
MESH = pl.DeviceIdType.MESH
F32 = jnp.float32
BF16 = jnp.bfloat16
CORNERS = ((-1, -1), (-1, 1), (1, -1), (1, 1))


def moments(g):
    def pair(lo, hi):
        return lo + hi, hi - lo

    s0 = [[None] * 3 for _ in range(3)]
    s1 = [[None] * 3 for _ in range(3)]
    s2 = [[None] * 3 for _ in range(3)]
    for a in range(3):
        for b in range(3):
            lo, mid, hi = g(a, b, 0), g(a, b, 1), g(a, b, 2)
            s2[a][b], s1[a][b] = pair(lo, hi)
            s0[a][b] = 4.0 * mid + s2[a][b]
    t00, t10, t20, t01, t11, t02 = [], [], [], [], [], []
    for a in range(3):
        ends, gap = pair(s0[a][0], s0[a][2])
        t00.append(4.0 * s0[a][1] + ends)
        t10.append(gap)
        t20.append(ends)
        ends, gap = pair(s1[a][0], s1[a][2])
        t01.append(4.0 * s1[a][1] + ends)
        t11.append(gap)
        t02.append(4.0 * s2[a][1] + (s2[a][0] + s2[a][2]))

    def whole(t):
        return 4.0 * t[1] + (t[0] + t[2])

    m200 = t00[0] + t00[2]
    return {
        "000": 4.0 * t00[1] + m200,
        "100": t00[2] - t00[0],
        "200": m200,
        "010": whole(t10),
        "110": t10[2] - t10[0],
        "020": whole(t20),
        "001": whole(t01),
        "101": t01[2] - t01[0],
        "011": whole(t11),
        "002": whole(t02),
    }


def line(o0, o1, o2, v):
    if o1 is None:
        d = v * o0
        e = o2 + v * d
    else:
        d = o1 + v * o0
        e = o2 + v * (o1 + d)
    return e - d, 0.5 * (o0 - e), e + d


def odd_line(o1, v):
    c = v * o1
    e = c + c
    return e - o1, -c, e + o1


def collided(m, omega):
    inv_m = 1.0 / m["000"]
    ux, uy, uz = m["100"] * inv_m, m["010"] * inv_m, m["001"] * inv_m
    n = {k: 0.125 * v for k, v in m.items()}
    rho, mx, my, mz = n["000"], n["100"], n["010"], n["001"]
    inverse = 8.0 * inv_m
    retain = 1.0 - omega
    c200 = n["200"] - mx * ux
    c020 = n["020"] - my * uy
    c002 = n["002"] - mz * uz
    third = 1.0 / 3.0
    d1 = retain * (c200 - c020)
    d2 = retain * (c200 - c002)
    total = rho + d1 + d2
    kxx = total * third
    kyy = (total - 3.0 * d1) * third
    kzz = (total - 3.0 * d2) * third
    kxy = retain * (n["110"] - mx * uy)
    kxz = retain * (n["101"] - mx * uz)
    kyz = retain * (n["011"] - my * uz)
    sxy, sxz, syz = kxy * kxy, kxz * kxz, kyz * kyz
    xy_xz, xy_yz, xz_yz = kxy * kxz, kxy * kyz, kxz * kyz
    k220 = (kxx * kyy + 2.0 * sxy) * inverse
    k202 = (kxx * kzz + 2.0 * sxz) * inverse
    yy_zz = kyy * kzz
    k022 = (yy_zz + 2.0 * syz) * inverse
    k211 = (kxx * kyz + 2.0 * xy_xz) * inverse
    k121 = (kyy * kxz + 2.0 * xy_yz) * inverse
    k112 = (kzz * kxy + 2.0 * xz_yz) * inverse
    k222 = (
        kxx * (yy_zz + 2.0 * syz) + 2.0 * (kyy * sxz + kzz * sxy) + 8.0 * (kxy * xz_yz)
    ) * (inverse * inverse)
    cols = {
        (0, 0): line(rho, None, kxx, ux),
        (1, 0): odd_line(kxy, ux),
        (2, 0): line(kyy, None, k220, ux),
        (0, 1): odd_line(kxz, ux),
        (1, 1): line(kyz, None, k211, ux),
        (2, 1): odd_line(k121, ux),
        (0, 2): line(kzz, None, k202, ux),
        (1, 2): odd_line(k112, ux),
        (2, 2): line(k022, None, k222, ux),
    }
    for a in range(3):
        by_y = [line(cols[0, c][a], cols[1, c][a], cols[2, c][a], uy) for c in range(3)]
        for b in range(3):
            ends = line(by_y[0][b], by_y[1][b], by_y[2][b], uz)
            for c in range(3):
                yield 9 * a + 3 * b + c, ends[c]


def kernel(
    n_gx,
    n_gy,
    count_ref,
    site_ref,
    patch_ref,
    pop_hbm,
    omega_hbm,
    walls_hbm,
    rad_hbm,
    bins_hbm,
    adv_ref,
    sig_ref,
    f_ref,
    rel,
    omega,
    walls,
    rad,
    bins,
    xsend,
    xrecv,
    ystage,
    ysend,
    yrecv,
    csend,
    crecv,
    lv_own,
    lv_gy,
    lv_sum,
    lv_in,
    one_hot,
    fields,
    rows,
    resp,
    resp_in,
    load_sem,
    halo_send,
    halo_recv,
    lvg_send,
    lvg_recv,
    lva_send,
    lva_recv,
    row_send,
    row_recv,
    resp_send,
    resp_recv,
):
    me_x, me_y = lax.axis_index("gx"), lax.axis_index("gy")

    def at_x(d):
        return lax.rem(me_x + (d + n_gx), n_gx)

    def at_y(d):
        return lax.rem(me_y + (d + n_gy), n_gy)

    layers = (3, 0, 1, 2)
    pop_loads = [
        pltpu.make_async_copy(pop_hbm.at[:, x], f_ref.at[:, x], load_sem.at[x]) for x in range(CX)
    ]
    omega_load = pltpu.make_async_copy(omega_hbm, omega, load_sem.at[4])
    walls_load = pltpu.make_async_copy(walls_hbm, walls, load_sem.at[5])
    bins_load = pltpu.make_async_copy(
        bins_hbm.at[:, pl.ds(pl.multiple_of(me_y * COLUMN, COLUMN), COLUMN)], bins, load_sem.at[6]
    )
    rad_load = pltpu.make_async_copy(rad_hbm.at[:, me_y], rad, load_sem.at[7])
    bins_load.start()
    omega_load.start()
    walls_load.start()
    for x in layers:
        pop_loads[x].start()
    rad_load.start()

    barrier = pltpu.get_barrier_semaphore()

    @pl.loop(1, n_gx)
    def _(d):
        pl.semaphore_signal(barrier, inc=1, device_id=(at_x(d), me_y), device_id_type=MESH)

    for e in range(1, n_gy):
        pl.semaphore_signal(barrier, inc=1, device_id=(me_x, at_y(e)), device_id_type=MESH)
    for sx, sy in CORNERS:
        pl.semaphore_signal(barrier, inc=1, device_id=(at_x(sx), at_y(sy)), device_id_type=MESH)

    def collide(s, first, layers):
        @pl.loop(0, 4 * layers)
        def _(j):
            x = first + j // 4
            y0 = pl.multiple_of(((j // 2) % 2) * 8, 8)
            z0 = pl.multiple_of((j % 2) * 128, 128)

            def g(a, b, c):
                return f_ref[9 * a + 3 * b + c, x, pl.ds(y0, 8), pl.ds(z0, 128)]

            m = moments(g)
            solid = walls[x, pl.ds(y0, 8), pl.ds(z0, 128)] == 1
            if s == 1:
                put_fields(m, x, y0, j % 2)
            for i, value in collided(m, omega[x, pl.ds(y0, 8), pl.ds(z0, 128)]):
                rel[s, i, x + 1, pl.ds(y0 + 8, 8), pl.ds(z0, 128)] = jnp.where(solid, WALL, value)

    def put_fields(m, x, y0, half):
        row = pl.multiple_of(half * 64 + x * CY + y0, 8)
        scale = 1.0 / 216.0
        fields[0, pl.ds(row, 8), :] = m["000"] * scale - 1.0
        fields[1, pl.ds(row, 8), :] = m["100"] * scale
        fields[2, pl.ds(row, 8), :] = m["010"] * scale
        fields[3, pl.ds(row, 8), :] = m["001"] * scale

    def x_copy(s, side):
        sx = 2 * side - 1
        return pltpu.make_async_remote_copy(
            src_ref=xsend.at[s, side],
            dst_ref=xrecv.at[s, side],
            send_sem=halo_send.at[s, side],
            recv_sem=halo_recv.at[s, side],
            device_id=(at_x(sx), me_y),
            device_id_type=MESH,
        )

    def y_copy(s, side):
        sy = 2 * side - 1
        return pltpu.make_async_remote_copy(
            src_ref=ysend.at[s, side],
            dst_ref=yrecv.at[s, side],
            send_sem=halo_send.at[s, 2 + side],
            recv_sem=halo_recv.at[s, 2 + side],
            device_id=(me_x, at_y(sy)),
            device_id_type=MESH,
        )

    def c_copy(s, corner):
        sx, sy = CORNERS[corner]
        return pltpu.make_async_remote_copy(
            src_ref=csend.at[s, corner, pl.ds(0, 3)],
            dst_ref=crecv.at[s, corner, pl.ds(0, 3)],
            send_sem=halo_send.at[s, 4 + corner],
            recv_sem=halo_recv.at[s, 4 + corner],
            device_id=(at_x(sx), at_y(sy)),
            device_id_type=MESH,
        )

    def crossing(sy):
        return [9 * a + 3 * (sy + 1) + c for a in range(3) for c in range(3)]

    def send_x(s, side):
        for j in range(9):
            value = rel[s, 18 * side + j, 1 + 3 * side, pl.ds(8, CY), :]
            xsend[s, side, j] = (value - 1.0).astype(BF16)
        x_copy(s, side).start()

    def send_y(s):
        for side in range(2):
            edge = 8 + 15 * side
            for j, i in enumerate(crossing(2 * side - 1)):
                for x in range(CX):
                    at = 4 * j + x
                    ystage[side, at : at + 1, :] = rel[s, i, x + 1, edge : edge + 1, :]
            ysend[s, side] = (ystage[side] - 1.0).astype(BF16)
            y_copy(s, side).start()

    def send_corners(s):
        for corner, (sx, sy) in enumerate(CORNERS):
            edge = 23 if sy > 0 else 8
            x = 4 if sx > 0 else 1
            for c in range(3):
                i = 9 * (sx + 1) + 3 * (sy + 1) + c
                csend[s, corner, c : c + 1, :] = rel[s, i, x, edge : edge + 1, :]
            c_copy(s, corner).start()

    def take_y(s):
        for side in range(2):
            y_copy(s, side).wait()
            ystage[side] = yrecv[s, side].astype(F32) + 1.0
            edge = 7 if side == 1 else 24
            for j, i in enumerate(crossing(2 * side - 1)):
                for x in range(CX):
                    at = 4 * j + x
                    rel[s, i, x + 1, edge : edge + 1, :] = ystage[side, at : at + 1, :]

    def take_x(s):
        for corner, (sx, sy) in enumerate(CORNERS):
            c_copy(s, corner).wait()
            edge = 7 if sy > 0 else 24
            x = 0 if sx > 0 else 5
            for c in range(3):
                i = 9 * (sx + 1) + 3 * (sy + 1) + c
                rel[s, i, x, edge : edge + 1, :] = crecv[s, corner, c : c + 1, :]
        for side in range(2):
            x_copy(s, side).wait()
            for j in range(9):
                rel[s, 18 * side + j, 5 - 5 * side, pl.ds(8, CY), :] = (
                    xrecv[s, side, j].astype(F32) + 1.0
                )

    def stream(s, first, step):
        to_ref = adv_ref if s == 1 else f_ref

        @pl.loop(0, 2)
        def _(j):
            x = first + j * step
            solid = walls[x] == 1
            for i in range(27):
                cx, cy, cz = i // 9 - 1, (i // 3) % 3 - 1, i % 3 - 1
                source = rel[s, i, x + 1 - cx, pl.ds(8 - cy, CY), :]
                if cz:
                    source = pltpu.roll(source, cz % NZ, 1)
                bounced = jnp.where(
                    source > WALL_TEST, rel[s, 26 - i, x + 1, pl.ds(8, CY), :], source
                )
                to_ref[i, x] = jnp.where(solid, f_ref[i, x], bounced)

    def late_fields(first, step):
        @pl.loop(0, 8)
        def _(j):
            x = first + (j // 4) * step
            y0 = pl.multiple_of(((j // 2) % 2) * 8, 8)
            z0 = pl.multiple_of((j % 2) * 128, 128)

            def g(a, b, c):
                return adv_ref[9 * a + 3 * b + c, x, pl.ds(y0, 8), pl.ds(z0, 128)]

            put_fields(moments(g), x, y0, j % 2)

    def send_rows(s):
        for part in range(4):
            taken = jnp.dot(selector, fields[part].astype(BF16), preferred_element_type=F32)
            rows[s, me_y, :, part * ZS : (part + 1) * ZS] = taken.astype(BF16)
        for e in range(1, n_gy):
            row_copy(s, e).start()

    def row_copy(s, e):
        return pltpu.make_async_remote_copy(
            src_ref=rows.at[s, me_y],
            dst_ref=rows.at[s, me_y],
            send_sem=row_send.at[s, e],
            recv_sem=row_recv.at[s, e],
            device_id=(me_x, at_y(e)),
            device_id_type=MESH,
        )

    def take_rows(s):
        for e in range(1, n_gy):
            pltpu.make_async_remote_copy(
                src_ref=rows.at[s, me_y],
                dst_ref=rows.at[s, at_y(-e)],
                send_sem=row_send.at[s, e],
                recv_sem=row_recv.at[s, e],
                device_id=(me_x, at_y(e)),
                device_id_type=MESH,
            ).wait()

    def lvg_copy(e):
        return pltpu.make_async_remote_copy(
            src_ref=lv_own,
            dst_ref=lv_gy.at[e],
            send_sem=lvg_send.at[e],
            recv_sem=lvg_recv.at[e],
            device_id=(me_x, at_y(e)),
            device_id_type=MESH,
        )

    def lva_copy(d):
        return pltpu.make_async_remote_copy(
            src_ref=lv_sum.at[at_x(d)],
            dst_ref=lv_in.at[d],
            send_sem=lva_send.at[d],
            recv_sem=lva_recv.at[d],
            device_id=(at_x(d), me_y),
            device_id_type=MESH,
        )

    def resp_copy(d):
        return pltpu.make_async_remote_copy(
            src_ref=resp.at[at_x(d)],
            dst_ref=resp_in.at[d],
            send_sem=resp_send.at[d],
            recv_sem=resp_recv.at[d],
            device_id=(at_x(d), me_y),
            device_id_type=MESH,
        )

    omega_load.wait()
    walls_load.wait()
    pop_loads[3].wait()
    collide(0, 3, 1)
    pl.semaphore_wait(barrier, n_gx - 1 + n_gy - 1 + 4)
    send_x(0, 1)
    pop_loads[0].wait()
    collide(0, 0, 1)
    send_x(0, 0)
    pop_loads[1].wait()
    pop_loads[2].wait()
    collide(0, 1, 2)
    send_y(0)
    send_corners(0)

    take_y(0)
    stream(0, 1, 1)
    collide(1, 1, 2)

    lane = lax.broadcasted_iota(jnp.int32, (COLUMN, 128), 1)
    sub = lax.broadcasted_iota(jnp.int32, (COLUMN, 128), 0)
    slot_patch = jnp.full((COLUMN, 128), -1, jnp.int32)
    for k in range(SAMP):
        local = patch_ref[0, k] - me_y * COLUMN
        slot_patch = jnp.where(lane % 64 == me_y * SAMP + k, local, slot_patch)
    pick = (slot_patch == sub).astype(BF16)
    bins_load.wait()
    level = lax.dot_general(
        bins[...].astype(F32).astype(BF16), pick, (((1,), (0,)), ((), ())), preferred_element_type=F32
    )
    lane_b = lax.broadcasted_iota(jnp.int32, (n_gx, 128), 1)
    later = (lane_b >= 64) & ((lane_b % 64) // SAMP == me_y)
    level = level + jnp.where(later, 1.0, 0.0)
    for b in range(n_gx):
        lv_own[b] = level[b : b + 1, :]
    for e in range(1, n_gy):
        lvg_copy(e).start()

    sub_k = lax.broadcasted_iota(jnp.int32, (SAMP, 128), 0)
    lane_k = lax.broadcasted_iota(jnp.int32, (SAMP, 128), 1)
    target = jnp.full((SAMP, 128), -1, jnp.int32)
    for k in range(SAMP):
        site = site_ref[0, k]
        target = jnp.where(sub_k == k, (site % 2) * 64 + site // 2, target)
    live = (target == lane_k) & (sub_k < count_ref[0, 0])
    selector = live.astype(BF16)

    take_x(0)
    stream(0, 0, 3)
    collide(1, 3, 1)
    send_x(1, 1)
    collide(1, 0, 1)
    send_x(1, 0)
    send_y(1)
    send_corners(1)
    send_rows(0)

    summed = lv_own[...]
    for e in range(1, n_gy):
        lvg_copy(e).wait()
        summed = summed + lv_gy[e]
    lv_sum[...] = summed

    @pl.loop(1, n_gx)
    def _(d):
        lva_copy(d).start()

    lv_in[0] = lv_sum[me_x]
    take_rows(0)
    rad_load.wait()
    take_y(1)
    stream(1, 1, 1)
    late_fields(1, 1)
    take_x(1)
    stream(1, 0, 3)
    late_fields(0, 3)
    send_rows(1)
    take_rows(1)
    all_rows = rows[...].reshape(2 * n_gy * SAMP, 4 * ZS)

    seen = lax.dot_general(
        rad[...].reshape(n_gx * OWN, 4 * ZS),
        all_rows,
        (((1,), (1,)), ((), ())),
        preferred_element_type=F32,
    )
    resp[...] = seen.astype(BF16).reshape(n_gx, OWN, 128)

    @pl.loop(1, n_gx)
    def _(d):
        resp_copy(d).start()

    resp_in[0] = resp[me_x]

    @pl.loop(0, n_gx)
    def _(d):
        @pl.when(d > 0)
        def _():
            lva_copy(d).wait()

        wanted = lax.broadcasted_iota(jnp.int32, (LEVELS, 128), 0).astype(F32)
        one_hot[d] = (jnp.broadcast_to(lv_in[d], (LEVELS, 128)) == wanted).astype(BF16)

    per = max(n_gx // 8, 1)
    total = jnp.zeros((OWN, LEVELS), F32)
    for start in range(0, n_gx // 2, per):
        group = list(range(start, start + per)) + list(range(n_gx - start - per, n_gx - start))
        for d in group:
            if d > 0:
                resp_copy(d).wait()
        total = total + lax.dot_general(
            jnp.concatenate([resp_in[d] for d in group], axis=1),
            jnp.concatenate([one_hot[d] for d in group], axis=1),
            (((1,), (1,)), ((), ())),
            preferred_element_type=F32,
        )
    sig_ref[...] = total


def finish(adv_in, sig_in, adv_out, sig_out, sem):
    copies = [
        pltpu.make_async_copy(adv_in.at[pl.ds(9 * a, 9)], adv_out.at[pl.ds(9 * a, 9)], sem.at[a])
        for a in range(3)
    ]
    copies.append(pltpu.make_async_copy(sig_in, sig_out, sem.at[3]))
    for copy in copies:
        copy.start()
    for copy in copies:
        copy.wait()


def per_device(populations, omega, walls, radiation, bins, counts, sample_site, sample_patch):
    n_gx, n_gy = lax.axis_size("gx"), lax.axis_size("gy")
    hbm = pl.BlockSpec(memory_space=pl.ANY)
    smem = pl.BlockSpec(memory_space=pltpu.SMEM)
    vmem = pl.BlockSpec(memory_space=pltpu.VMEM)
    dma = pltpu.SemaphoreType.DMA
    scratch = [
        pltpu.VMEM((27, CX, CY, NZ), F32),
        pltpu.VMEM((2, 27, CX + 2, CY + 16, NZ), F32),
        pltpu.VMEM((CX, CY, NZ), F32),
        pltpu.VMEM((CX, CY, NZ), jnp.int32),
        pltpu.VMEM((n_gx, OWN, 4 * ZS), BF16),
        pltpu.VMEM((n_gx, COLUMN), jnp.int32),
        pltpu.VMEM((2, 2, 9, CY, NZ), BF16),
        pltpu.VMEM((2, 2, 9, CY, NZ), BF16),
        pltpu.VMEM((2, 9 * CX, NZ), F32),
        pltpu.VMEM((2, 2, 9 * CX, NZ), BF16),
        pltpu.VMEM((2, 2, 9 * CX, NZ), BF16),
        pltpu.VMEM((2, 4, 8, NZ), F32),
        pltpu.VMEM((2, 4, 8, NZ), F32),
        pltpu.VMEM((n_gx, 1, 128), F32),
        pltpu.VMEM((n_gy, n_gx, 1, 128), F32),
        pltpu.VMEM((n_gx, 1, 128), F32),
        pltpu.VMEM((n_gx, 1, 128), F32),
        pltpu.VMEM((n_gx, LEVELS, 128), BF16),
        pltpu.VMEM((4, 128, ZS), F32),
        pltpu.VMEM((2, n_gy, SAMP, 4 * ZS), BF16),
        pltpu.VMEM((n_gx, OWN, 128), BF16),
        pltpu.VMEM((n_gx, OWN, 128), BF16),
        dma((8,)),
        dma((2, 8)),
        dma((2, 8)),
        dma((n_gy,)),
        dma((n_gy,)),
        dma((n_gx,)),
        dma((n_gx,)),
        dma((2, n_gy)),
        dma((2, n_gy)),
        dma((n_gx,)),
        dma((n_gx,)),
    ]
    operands = (
        sample_site.reshape(1, SAMP),
        sample_patch.reshape(1, SAMP),
        populations,
        omega,
        walls,
        radiation.reshape(n_gx, n_gy, OWN, 4 * ZS),
        bins.T,
    )
    advanced, signal = pl.pallas_call(
        functools.partial(kernel, n_gx, n_gy),
        out_shape=(
            jax.ShapeDtypeStruct((27, CX, CY, NZ), F32),
            jax.ShapeDtypeStruct((OWN, LEVELS), F32),
        ),
        in_specs=[smem] * 3 + [hbm] * 5,
        out_specs=(vmem, vmem),
        scratch_shapes=scratch,
        compiler_params=pltpu.CompilerParams(
            collective_id=0, has_side_effects=True, vmem_limit_bytes=44 * 2**20
        ),
        name="lattice_far_field",
    )(counts, *[pltpu.with_memory_space_constraint(x, pltpu.HBM) for x in operands])
    return pl.pallas_call(
        finish,
        out_shape=(
            jax.ShapeDtypeStruct((27, CX, CY, NZ), F32),
            jax.ShapeDtypeStruct((OWN, LEVELS), F32),
        ),
        in_specs=[hbm] * 2,
        out_specs=(hbm, hbm),
        scratch_shapes=[dma((4,))],
        compiler_params=pltpu.CompilerParams(vmem_limit_bytes=2**20),
        name="write_out",
    )(advanced, signal)


def solution(mesh):
    return jax.shard_map(
        per_device,
        mesh=mesh,
        in_specs=(
            P(None, "gx", "gy", None),
            P("gx", "gy", None),
            P("gx", "gy", None),
            P(),
            P(),
            P("gx", "gy"),
            P("gx", "gy", None),
            P("gx", "gy", None),
        ),
        out_specs=(P(None, "gx", "gy", None), P(("gx", "gy"), None)),
        check_vma=False,
    )
```
